32 devices in a mesh: sec: 8 (over y, x, core), mode: 4 (over z).
Axes of the slice: x: 2, y: 2, z: 4, core: 2. Of those that a mesh axis runs over, the one named last changes fastest.
Arguments:
- coupling: float32 [8, 512, 512], P('sec'), may hold values from -1.25 to 0.25
- stiffness: float32 [8, 512, 512], P('sec'), may hold values from -0.5 to 3.5, as said below
- loads: float32 [8, 16, 512], P('sec'), may hold values from -60 to 60
- modes: bfloat16 [8, 512, 1024], P('sec', None, 'mode'), may hold values from -0.09375 to 0.09375
- joint_section: int32 [8192], P('sec'), may hold values from 0 to 7
- regime: int32 [128], P('sec'), may hold values from 0 to 3
- participation: bfloat16 [8192, 1024], P('sec', 'mode'), may hold values from -0.0625 to 0.0625
Outputs:
- displacement: float32 [8, 16, 512], P('sec', None, 'mode')
- motion: float32 [8, 16, 512], P('sec', None, 'mode')
The draws below stay inside these ranges and needn't reach their ends.
Inputs may be any that keep to these rules, and one draw needn't show every extreme that they name: Each section's block is symmetric, and the whole block-tridiagonal operator built from stiffness and coupling is symmetric positive definite.
All inputs are finite; a program needn't handle non-finite values.
Results may differ from the reference program's by a relative error of at most 0.00047.
Values sent between devices are 32-bit elements; how exact they have to be, the bound alone decides.
No kernel may reach another device: no remote copies, remote signals or barrier semaphores. Data moves between devices by JAX's collectives and lax.ppermute only.
A program may use at most 64 MiB of HBM per device.

```python
import jax
import jax.numpy as jnp
from jax import lax

M = 512
K = 16
NMODES = 1024
LEVELS = 3
INVERSE_STEPS = 3
BUCKET = 64
SECS = 8
JOINTS = 8192


def draw_coupling(key, part):
    key_diag = jax.random.fold_in(key, 31)
    key_noise = jax.random.fold_in(key, 32)
    diagonal = jax.random.uniform(key_diag, (SECS, M), jnp.float32, 0.95, 1.15)
    noise_part = jnp.clip(jax.random.normal(key_noise, (SECS, M, M), jnp.float32), -3.0, 3.0) * (0.08 / M ** 0.5)
    return noise_part - diagonal[:, :, None] * jnp.eye(M, dtype=jnp.float32)[None, :, :]


def draw_stiffness(key, part):
    key_diag = jax.random.fold_in(key, 11)
    key_noise = jax.random.fold_in(key, 12)
    diagonal = jax.random.uniform(key_diag, (SECS, M), jnp.float32, 2.7, 3.0)
    spread = 0.24
    noise_part = jax.random.uniform(key_noise, (SECS, M, M), jnp.float32, -1.0, 1.0) * (spread / M ** 0.5)
    symmetric = 0.5 * (noise_part + jnp.swapaxes(noise_part, 1, 2))
    return symmetric + diagonal[:, :, None] * jnp.eye(M, dtype=jnp.float32)[None, :, :]


def draw_loads(key, part):
    key_section = jax.random.fold_in(key, 21)
    key_column = jax.random.fold_in(key, 22)
    key_base = jax.random.fold_in(key, 23)
    section_scale = jnp.exp(jax.random.uniform(key_section, (SECS, 1, 1), jnp.float32, jnp.log(0.5), jnp.log(5.0)))
    column_scale = jnp.exp(jax.random.uniform(key_column, (1, K, 1), jnp.float32, jnp.log(0.5), jnp.log(2.0)))
    base_part = jnp.clip(jax.random.normal(key_base, (SECS, K, M), jnp.float32), -6.0, 6.0)
    return base_part * section_scale * column_scale


def place_ends(result, own_key, smallest, high):
    place = [jax.random.randint(jax.random.fold_in(own_key, axis), (), 0, length) for axis, length in enumerate(result.shape)]
    widest = result.shape.index(max(result.shape))
    neighbour = place[:widest] + [(place[widest] + 1) % result.shape[widest]] + place[widest + 1:]
    return result.at[tuple(place)].set(smallest).at[tuple(neighbour)].set(high)


def level_of(rng, dims, shards, least, top_value):
    factor_of, own = 1.0, jax.random.fold_in(rng, 6)
    for axis_at, shards_of in shards:
        heights = jnp.exp(jax.random.uniform(jax.random.fold_in(own, axis_at), (shards_of,), jnp.float32, least / len(shards), top_value / len(shards)))
        factor_of = factor_of * jnp.repeat(heights, dims[axis_at] // shards_of).reshape([-1 if axis == axis_at else 1 for axis in range(len(dims))])
    return factor_of


def bell_draw(key, extent, scale, most, shards=(), held_as=jnp.bfloat16):
    values = scale * jax.random.normal(key, extent, jnp.float32)
    if shards:
        values = values * level_of(key, extent, shards, -0.22, 0.18)
    return jnp.clip(values, -most, most).astype(held_as)


def setup_inputs(seed: int = 0) -> dict:
    splits = jax.random.split(jax.random.key(seed), 8)
    coupling = draw_coupling(jax.random.fold_in(splits[7], 71), 0)
    stiffness = draw_stiffness(jax.random.fold_in(splits[7], 71), 0)
    loads = draw_loads(jax.random.fold_in(splits[7], 71), 0)
    modes = bell_draw(splits[3], (SECS, M, NMODES), (SECS * M) ** -0.5, 0.09375, ((0, 8), (2, 4)))
    joint_section = place_ends(jax.random.randint(splits[4], (JOINTS,), 0, SECS), jax.random.fold_in(splits[4], 1), 0, SECS - 1).astype(jnp.int32)
    regime = place_ends(jax.random.randint(splits[5], (JOINTS // BUCKET,), 0, 4), jax.random.fold_in(splits[5], 1), 0, 3).astype(jnp.int32)
    participation = bell_draw(splits[6], (JOINTS, NMODES), JOINTS ** -0.5, 0.0625, ((0, 8), (1, 4)))
    return dict(coupling=coupling, stiffness=stiffness, loads=loads, modes=modes, joint_section=joint_section, regime=regime, participation=participation)


def invert(blocks):
    highest = lax.Precision.HIGHEST
    diagonal = jnp.diagonal(blocks, axis1=1, axis2=2)
    inverse = jnp.eye(M, dtype=jnp.float32)[None, :, :] * (1.0 / diagonal)[:, :, None]
    for inner_step in range(INVERSE_STEPS):
        product = jnp.einsum('sij,sjk->sik', blocks, inverse, precision=highest)
        inverse = 2.0 * inverse - jnp.einsum('sij,sjk->sik', inverse, product, precision=highest)
    return inverse

def shift_down(array, distance):
    return jnp.concatenate([jnp.zeros_like(array[:distance]), array[:-distance]], axis=0)

def shift_up(array, distance):
    return jnp.concatenate([array[distance:], jnp.zeros_like(array[:distance])], axis=0)

def reference(coupling, stiffness, loads, modes, joint_section, regime, participation):
    highest = lax.Precision.HIGHEST
    sections = jnp.arange(SECS)
    coupling_now = coupling * (sections >= 1).astype(jnp.float32)[:, None, None]
    blocks = stiffness
    right_side = jnp.swapaxes(loads, 1, 2)
    for reduction_level in range(LEVELS):
        distance = 2 ** reduction_level
        inverse = invert(blocks)
        inv_lower = jnp.einsum('sij,sjk->sik', inverse, coupling_now, precision=highest)
        inv_rhs = jnp.einsum('sij,sjk->sik', inverse, right_side, precision=highest)
        upper_sum = jnp.einsum('sji,sjk->sik', coupling_now, inv_lower, precision=highest)
        upper_rhs = jnp.einsum('sji,sjk->sik', coupling_now, inv_rhs, precision=highest)
        inverse_down = shift_down(inverse, distance)
        lower_down = shift_down(inv_lower, distance)
        rhs_down = shift_down(inv_rhs, distance)
        sum_up = shift_up(upper_sum, distance)
        rhs_up = shift_up(upper_rhs, distance)
        through = jnp.einsum('sij,sjk->sik', coupling_now, inverse_down, precision=highest)
        blocks = blocks - jnp.einsum('sij,skj->sik', through, coupling_now, precision=highest) - sum_up
        right_side = right_side - jnp.einsum('sij,sjk->sik', coupling_now, rhs_down, precision=highest) - rhs_up
        coupling_now = -jnp.einsum('sij,sjk->sik', coupling_now, lower_down, precision=highest)
    inverse = invert(blocks)
    solution = jnp.einsum('sij,sjk->sik', inverse, right_side, precision=highest)
    displacement = jnp.swapaxes(solution, 1, 2)
    rounded = displacement.astype(jnp.bfloat16)
    mode_values = modes.astype(jnp.float32)
    modal_coords = jnp.einsum('skm,smn->kn', rounded.astype(jnp.float32), mode_values, precision=highest)
    amplitude = jnp.sqrt(lax.optimization_barrier(jnp.mean(displacement * displacement, axis=(1, 2))) + 1e-06)
    joint_regime = jnp.repeat(regime, BUCKET)
    joint_rate = jnp.array([0.2, 0.5, 1.0, 2.0], dtype=jnp.float32)[joint_regime]
    local_amplitude = amplitude[joint_section]
    strength = joint_rate * local_amplitude / (1.0 + local_amplitude)
    weights = participation.astype(jnp.float32)
    damping = jnp.dot(strength, weights * weights, precision=highest)
    damped_share = damping / (1.0 + damping)
    removed = (modal_coords * damped_share[None, :]).astype(jnp.bfloat16)
    returned = jnp.einsum('kn,smn->skm', removed.astype(jnp.float32), mode_values, precision=highest)
    motion = displacement - returned
    return (displacement, motion)
```

```python
import functools

import jax
import jax.numpy as jnp
from jax import lax
from jax.experimental import pallas as pl
from jax.experimental.pallas import tpu as pltpu
from jax.sharding import PartitionSpec as P

LEVELS = 3
BUCKET = 64
RATES = (0.2, 0.5, 1.0, 2.0)
AXES = ("sec", "mode")
TILE = 128
f32, bf16 = jnp.float32, jnp.bfloat16


def split(value):
    high = value.astype(bf16)
    return high, (value - high.astype(f32)).astype(bf16)


def dot(left, right):
    return jnp.dot(left, right, preferred_element_type=f32)


def dot_t(left, right):
    return lax.dot_general(left, right, (((1,), (1,)), ((), ())), preferred_element_type=f32)


def times(left, right, product=dot):
    return product(left[0], right[0]) + product(left[0], right[1]) + product(left[1], right[0])


def upper(size):
    count = size // TILE
    return [(a, b) for a in range(count) for b in range(a, count)]


def band(index):
    return slice(TILE * index, TILE * index + TILE)


def unpack(packed, block, thin):
    size = block.shape[0]
    cells = upper(size)
    for index, (a, b) in enumerate(cells):
        cell = packed[band(index), :]
        block[band(a), band(b)] = cell
        if a != b:
            block[band(b), band(a)] = cell.T
    rows = thin.shape[0]
    for c in range(size // TILE):
        start = TILE * len(cells) + rows * c
        thin[:, band(c)] = packed[start : start + rows, :]


def pack(packed, block, thin):
    size = block.shape[1]
    cells = upper(size)
    for index, (a, b) in enumerate(cells):
        packed[band(index), :] = block[band(a), band(b)]
    rows = thin.shape[0]
    for c in range(size // TILE):
        start = TILE * len(cells) + rows * c
        packed[start : start + rows, :] = thin[:, band(c)]


def scaled(block):
    size = block.shape[0]
    eye = lax.broadcasted_iota(jnp.int32, (size, size), 0) == lax.broadcasted_iota(
        jnp.int32, (size, size), 1
    )
    only = jnp.where(eye, block, 0.0)
    down = jnp.sum(only, axis=1, keepdims=True)
    along = jnp.sum(only, axis=0, keepdims=True)
    down = jnp.where(down == 0.0, 0.0, 1.0 / down)
    along = jnp.where(along == 0.0, 0.0, 1.0 / along)
    unit = jnp.where(eye, 1.0, 0.0)
    return unit, down, along, unit - down * block


def inverse_of(block):
    unit, down, along, first = scaled(block)
    one = split(first)
    second = times(one, one)
    two = split(second)
    third = times(one, two)
    fourth = dot(two[0], two[0]).astype(bf16)
    series = unit + first + second + third
    series = series + dot(series.astype(bf16), fourth)
    return series * along


def schur(rows_and_thin, inverse, right, product):
    through = times(split(rows_and_thin), split(inverse))
    return through, times(split(through), split(right), product)


def pack_kernel(block, thin, packed):
    pack(packed, block, thin)


def own_kernel(block, thin, lower, packed, stack, out):
    size = block.shape[0]
    inverse = inverse_of(block[...])
    stack[0:size, :] = lower[...].T
    stack[size:, :] = thin[...]
    _, out[...] = schur(stack[...], inverse, lower[...], dot)
    pack(packed, out, out.at[size:, :])


def above_kernel(inverse, thin, lower, packed, stack, out):
    size = inverse.shape[0]
    stack[0:size, :] = lower[...].T
    stack[size:, :] = thin[...]
    _, out[...] = schur(stack[...], inverse[...], lower[...], dot)
    pack(packed, out, out.at[size:, :])


def receive_kernel(packed, lower, block, thin, above, through, out, stack, whole):
    size = block.shape[0]
    unpack(packed, whole, stack.at[size:, :])
    inverse = inverse_of(whole[...])
    stack[0:size, :] = lower[...]
    half, full = schur(stack[...], inverse, lower[...], dot_t)
    through[...] = half[0:size, :]
    stack[...] = full
    cells = upper(size)
    for index, (a, b) in enumerate(cells):
        out[band(index), :] = block[band(a), band(b)] - stack[band(a), band(b)] - above[band(index), :]
    rows = thin.shape[0]
    for c in range(size // TILE):
        start = TILE * len(cells) + rows * c
        out[start : start + rows, :] = (
            thin[:, band(c)] - stack[size:, band(c)] - above[start : start + rows, :]
        )


def invert_kernel(packed, inverse, block, thin):
    unpack(packed, block, thin)
    inverse[...] = inverse_of(block[...])


def lower_kernel(through, passed, lower):
    lower[...] = -times(split(through[...]), split(passed[...]))


def last_lower_kernel(through, passed, inverse, thin, lower, packed, stack, out):
    size = inverse.shape[0]
    value = -times(split(through[...]), split(passed[...]))
    lower[...] = value
    stack[0:size, :] = value.T
    stack[size:, :] = thin[...]
    _, out[...] = schur(stack[...], inverse[...], value, dot)
    pack(packed, out, out.at[size:, :])


def last_receive_kernel(inverse, thin_passed, lower, block, thin, block_out, thin_out, stack):
    size = block.shape[0]
    stack[0:size, :] = lower[...]
    stack[size:, :] = thin_passed[...]
    _, full = schur(stack[...], inverse[...], lower[...], dot_t)
    block_out[...] = block[...] - full[0:size, :]
    thin_out[...] = thin[...] - full[size:, :]


def solve_kernel(block, thin, above, solution, whole, own):
    unpack(above, whole, own)
    value = block[...] - whole[...]
    _, down, along, first = scaled(value)
    one = split(first)
    now = (thin[...] - own[...]) * along
    for power in (1, 2, 4):
        moved = now
        for _ in range(power):
            moved = times(split(moved), one, dot_t)
        now = now + moved
    solution[...] = now


def modal_kernel(a, b, c, d, modes, shares, whole, payload):
    value = a[...] + b[...] + c[...] + d[...]
    whole[...] = value
    amplitude = jnp.sqrt(jnp.sum(value * value, keepdims=True) / value.size + 1e-06)
    rows = value.shape[0]
    payload[...] = jnp.zeros_like(payload)
    payload[0:rows, :] = dot(value.astype(bf16), modes[...])
    payload[rows : rows + 1, :] = shares[...] * (amplitude / (1.0 + amplitude))


def back_kernel(place, mine, other, modes, *outs):
    total = mine[...] + other[...]
    scratch = outs[-1]
    pieces = outs[:-1]
    rows = scratch.shape[0]
    damping = total[rows : rows + 1, :]
    removed = (total[0:rows, :] * (damping / (1.0 + damping))).astype(bf16)
    scratch[...] = dot_t(removed, modes[...])
    width = pieces[0].shape[1]
    for k, piece in enumerate(pieces):
        start = lax.rem(place[0] + k, len(pieces)) * width
        piece[...] = scratch[:, pl.ds(pl.multiple_of(start, width), width)]


def call(kernel, outs, scratch, args, flops, smem=0):
    vmem, scalar = pl.BlockSpec(memory_space=pltpu.VMEM), pl.BlockSpec(memory_space=pltpu.SMEM)
    moved = sum(a.size * a.dtype.itemsize for a in args) + sum(4 * o[0] * o[1] for o in outs)
    single = len(outs) == 1
    shapes = [jax.ShapeDtypeStruct(o, f32) for o in outs]
    return pl.pallas_call(
        kernel,
        out_shape=shapes[0] if single else tuple(shapes),
        in_specs=[scalar] * smem + [vmem] * (len(args) - smem),
        out_specs=vmem if single else tuple([vmem] * len(outs)),
        scratch_shapes=[pltpu.VMEM(s, f32) for s in scratch],
        compiler_params=pltpu.CompilerParams(vmem_limit_bytes=40 << 20),
        cost_estimate=pl.CostEstimate(flops=flops, transcendentals=0, bytes_accessed=moved),
    )(*args)


def per_device(coupling, stiffness, loads, modes, joint_section, regime, participation):
    position, plane = lax.axis_index("sec"), lax.axis_index("mode")
    sections, groups = lax.axis_size("sec"), lax.axis_size("mode")
    size, columns = stiffness.shape[1], loads.shape[1]
    width = size // groups
    cells = len(upper(size))
    packed = (TILE * cells + columns * (size // TILE), TILE)
    square, stacked, thin_shape = (size, size), (size + columns, size), (columns, size)
    product = 6 * size**3

    def moved(value, step, level):
        stride = min(2 ** (level + 1), groups)
        pairs = []
        for target in range(sections):
            source = target - step
            if 0 <= source < sections:
                pairs += [
                    (source * groups + m, target * groups + m)
                    for m in range(groups)
                    if (target - m) % stride == 0
                ]
        return lax.ppermute(value, AXES, pairs)

    def exchanged(value, to, wanted=lambda s, m: True):
        pairs = []
        for s in range(sections):
            for m in range(groups):
                if wanted(s, m):
                    s_to, m_to = to(s, m)
                    pairs.append((s * groups + m, s_to * groups + m_to))
        return lax.ppermute(value, AXES, pairs)

    lower = coupling[0] * (position >= 1).astype(f32)
    block, thin = stiffness[0], loads[0]

    matches = (jnp.arange(sections, dtype=jnp.int32)[:, None] == joint_section[None, :]).astype(f32)
    joint_regime = jnp.broadcast_to(regime[:, None], (regime.shape[0], BUCKET)).reshape(-1)
    joint_rate = jnp.zeros(joint_regime.shape, f32)
    for value_index, rate_value in enumerate(RATES):
        joint_rate = joint_rate + (joint_regime == value_index).astype(f32) * rate_value
    weights = participation.astype(f32)
    shares = jnp.dot(
        matches * joint_rate[None, :], weights * weights, precision=lax.Precision.HIGHEST
    )

    sent = call(pack_kernel, [packed], [], (block, thin), 0)
    block_down = moved(sent, 1, 0)
    lower_down = moved(lower, 1, 0)
    up = call(own_kernel, [packed], [stacked, stacked], (block, thin, lower), 6 * product)
    up = moved(up, -1, 0)
    through, sent = call(
        receive_kernel, [square, packed], [stacked, square], (block_down, lower, block, thin, up), 6 * product
    )

    def unpacked(value):
        def kernel(packed_ref, block_ref, thin_ref):
            unpack(packed_ref, block_ref, thin_ref)

        return call(kernel, [square, thin_shape], [], (value,), 0)

    block_down = moved(sent, 2, 1)
    block, thin = unpacked(sent)
    inverse = call(invert_kernel, [square], [square, thin_shape], (sent,), 4 * product)
    lower = call(lower_kernel, [square], [], (through, lower_down), product)
    lower_down = moved(lower, 2, 1)
    up = call(above_kernel, [packed], [stacked, stacked], (inverse, thin, lower), 2 * product)
    up = moved(up, -2, 1)
    through, sent = call(
        receive_kernel, [square, packed], [stacked, square], (block_down, lower, block, thin, up), 6 * product
    )

    block_down = moved(sent, 4, 2)
    block, thin = unpacked(sent)
    inverse = call(invert_kernel, [square], [square, thin_shape], (sent,), 4 * product)
    lower, up = call(
        last_lower_kernel, [square, packed], [stacked, stacked], (through, lower_down, inverse, thin), 3 * product
    )
    up = moved(up, -4, 2)
    thin_down = unpacked(block_down)[1]
    inverse = call(invert_kernel, [square], [square, thin_shape], (block_down,), 4 * product)
    block, thin = call(
        last_receive_kernel, [square, thin_shape], [stacked], (inverse, thin_down, lower, block, thin), 2 * product
    )
    solved = call(solve_kernel, [thin_shape], [square, thin_shape], (block, thin, up), product)

    home = lambda s, m: m == s % groups
    parts = [
        exchanged(solved, lambda s, m, k=k: (s, (m + k) % groups), home) for k in range(1, groups)
    ]
    solved = jnp.where(lax.rem(position, groups) == plane, solved, 0.0)
    for bit in range(sections.bit_length() - 1):
        shares = shares + exchanged(shares, lambda s, m, bit=bit: (s ^ (1 << bit), m))
    shares = lax.dynamic_slice_in_dim(shares, position, 1, 0)
    padded = (columns + 8, modes.shape[2])
    whole, payload = call(
        modal_kernel, [thin_shape, padded], [], (solved, *parts, modes[0], shares), product // 32
    )
    for bit in range(sections.bit_length() - 1):
        other = exchanged(payload, lambda s, m, bit=bit: (s ^ (1 << bit), m))
        if bit < sections.bit_length() - 2:
            payload = payload + other
    pieces = call(
        back_kernel,
        [(columns, width)] * groups,
        [thin_shape],
        (plane.reshape(1), payload, other, modes[0]),
        product // 32,
        smem=1,
    )
    summed = pieces[0]
    for k in range(1, groups):
        summed = summed + exchanged(pieces[k], lambda s, m, k=k: (s, (m + k) % groups))
    own_columns = lax.dynamic_slice_in_dim(whole, plane * width, width, 1)
    return (own_columns[None], (own_columns - summed)[None])


def solution(mesh):
    in_specs = (
        P("sec", None, None),
        P("sec", None, None),
        P("sec", None, None),
        P("sec", None, "mode"),
        P("sec"),
        P("sec"),
        P("sec", "mode"),
    )
    out_specs = (P("sec", None, "mode"), P("sec", None, "mode"))
    return jax.shard_map(
        per_device, mesh=mesh, in_specs=in_specs, out_specs=out_specs, check_vma=False
    )
```

```python
import functools

import jax
import jax.numpy as jnp
from jax import lax
from jax.experimental import pallas as pl
from jax.experimental.pallas import tpu as pltpu
from jax.sharding import PartitionSpec as P

LEVELS = 3
BUCKET = 64
RATES = (0.2, 0.5, 1.0, 2.0)
AXES = ("sec", "mode")
TILE = 128
f32, bf16 = jnp.float32, jnp.bfloat16


def split(value):
    high = value.astype(bf16)
    return high, (value - high.astype(f32)).astype(bf16)


def dot(left, right):
    return jnp.dot(left, right, preferred_element_type=f32)


def dot_t(left, right):
    return lax.dot_general(left, right, (((1,), (1,)), ((), ())), preferred_element_type=f32)


def times(left, right, product=dot):
    return product(left[0], right[0]) + product(left[0], right[1]) + product(left[1], right[0])


def upper(size):
    count = size // TILE
    return [(a, b) for a in range(count) for b in range(a, count)]


def band(index):
    return slice(TILE * index, TILE * index + TILE)


def unpack(packed, block, thin):
    size = block.shape[0]
    cells = upper(size)
    for index, (a, b) in enumerate(cells):
        cell = packed[band(index), :]
        block[band(a), band(b)] = cell
        if a != b:
            block[band(b), band(a)] = cell.T
    rows = thin.shape[0]
    for c in range(size // TILE):
        start = TILE * len(cells) + rows * c
        thin[:, band(c)] = packed[start : start + rows, :]


def pack(packed, block, thin):
    size = block.shape[1]
    cells = upper(size)
    for index, (a, b) in enumerate(cells):
        packed[band(index), :] = block[band(a), band(b)]
    rows = thin.shape[0]
    for c in range(size // TILE):
        start = TILE * len(cells) + rows * c
        packed[start : start + rows, :] = thin[:, band(c)]


def scaled(block):
    size = block.shape[0]
    eye = lax.broadcasted_iota(jnp.int32, (size, size), 0) == lax.broadcasted_iota(
        jnp.int32, (size, size), 1
    )
    only = jnp.where(eye, block, 0.0)
    down = jnp.sum(only, axis=1, keepdims=True)
    along = jnp.sum(only, axis=0, keepdims=True)
    down = jnp.where(down == 0.0, 0.0, 1.0 / down)
    along = jnp.where(along == 0.0, 0.0, 1.0 / along)
    unit = jnp.where(eye, 1.0, 0.0)
    return unit, down, along, unit - down * block


def inverse_of(block):
    unit, down, along, first = scaled(block)
    one = split(first)
    second = times(one, one)
    two = split(second)
    third = times(one, two)
    fourth = dot(two[0], two[0]).astype(bf16)
    series = unit + first + second + third
    series = series + dot(series.astype(bf16), fourth)
    return series * along


def schur(rows_and_thin, inverse, right, product):
    through = times(split(rows_and_thin), split(inverse))
    return through, times(split(through), split(right), product)


def pack_kernel(block, thin, packed):
    pack(packed, block, thin)


def folded(packed, block, thin, *others):
    size = block.shape[0]
    cells = upper(size)
    for index, (a, b) in enumerate(cells):
        value = block[band(a), band(b)]
        for other in others:
            same = other.shape == packed.shape
            value = value - (other[band(index), :] if same else other[band(a), band(b)])
        packed[band(index), :] = value
    rows = thin.shape[0]
    for c in range(size // TILE):
        start = TILE * len(cells) + rows * c
        value = thin[:, band(c)]
        for other in others:
            same = other.shape == packed.shape
            value = value - (other[start : start + rows, :] if same else other[size:, band(c)])
        packed[start : start + rows, :] = value


def own_kernel(block, thin, lower, packed, stack, out):
    size = block.shape[0]
    inverse = inverse_of(block[...])
    stack[0:size, :] = lower[...].T
    stack[size:, :] = thin[...]
    _, out[...] = schur(stack[...], inverse, lower[...], dot)
    pack(packed, out, out.at[size:, :])


def receive_kernel(packed, lower, through, full, stack, whole):
    size = lower.shape[0]
    unpack(packed, whole, stack.at[size:, :])
    inverse = inverse_of(whole[...])
    stack[0:size, :] = lower[...]
    half, full[...] = schur(stack[...], inverse, lower[...], dot_t)
    through[...] = half[0:size, :]


def fold_kernel(block, thin, full, above, packed, block_out, thin_out):
    folded(packed, block, thin, full, above)
    unpack(packed, block_out, thin_out)


def fold_above_kernel(packed_above, passed, block, thin, full, packed, block_out, thin_out, stack, out, whole):
    size = block.shape[0]
    unpack(packed_above, whole, stack.at[size:, :])
    right = split(passed[...])
    stack[0:size, :] = times(split(passed[...].T), split(whole[...]))
    stack[size:, :] = -stack[size:, :]
    out[...] = times(split(stack[...]), right)
    folded(packed, block, thin, full, out)
    unpack(packed, block_out, thin_out)


def whole_inverse_kernel(block, inverse):
    inverse[...] = inverse_of(block[...])


def invert_kernel(packed, inverse, thin, block):
    unpack(packed, block, thin)
    inverse[...] = inverse_of(block[...])


def lower_kernel(through, passed, lower):
    lower[...] = -times(split(through[...]), split(passed[...]))


def last_lower_kernel(through, passed, inverse, thin, lower, packed, stack, out):
    size = inverse.shape[0]
    value = -times(split(through[...]), split(passed[...]))
    lower[...] = value
    stack[0:size, :] = value.T
    stack[size:, :] = thin[...]
    _, out[...] = schur(stack[...], inverse[...], value, dot)
    pack(packed, out, out.at[size:, :])


def last_receive_kernel(inverse, thin_passed, lower, block, thin, block_out, thin_out, stack):
    size = block.shape[0]
    stack[0:size, :] = lower[...]
    stack[size:, :] = thin_passed[...]
    _, full = schur(stack[...], inverse[...], lower[...], dot_t)
    block_out[...] = block[...] - full[0:size, :]
    thin_out[...] = thin[...] - full[size:, :]


def solve_kernel(block, thin, above, solution, whole, own):
    unpack(above, whole, own)
    value = block[...] - whole[...]
    unit, _, along, _ = scaled(value)
    high, low = split(unit - value * along)
    rows = thin.shape[0]
    now = (thin[...] - own[...]) * along
    for power in (1, 2, 4):
        moved = now
        for _ in range(power):
            top, rest = split(moved)
            both = dot(jnp.concatenate([top, rest], axis=0), high)
            moved = both[0:rows, :] + both[rows:, :] + dot(top, low)
        now = now + moved
    solution[...] = now


def modal_kernel(a, b, c, d, modes, shares, whole, payload):
    value = a[...] + b[...] + c[...] + d[...]
    whole[...] = value
    amplitude = jnp.sqrt(jnp.sum(value * value, keepdims=True) / value.size + 1e-06)
    rows = value.shape[0]
    payload[...] = jnp.zeros_like(payload)
    payload[0:rows, :] = dot(value.astype(bf16), modes[...])
    payload[rows : rows + 1, :] = shares[...] * (amplitude / (1.0 + amplitude))


def back_kernel_of(count, place, *refs):
    parts, modes, pieces, scratch = refs[:count], refs[count], refs[count + 1 : -1], refs[-1]
    total = parts[0][...]
    for part in parts[1:]:
        total = total + part[...]
    rows = scratch.shape[0]
    damping = total[rows : rows + 1, :]
    removed = (total[0:rows, :] * (damping / (1.0 + damping))).astype(bf16)
    scratch[...] = dot_t(removed, modes[...])
    width = pieces[0].shape[1]
    for k, piece in enumerate(pieces):
        start = lax.rem(place[0] + k, len(pieces)) * width
        piece[...] = scratch[:, pl.ds(pl.multiple_of(start, width), width)]


def call(kernel, outs, scratch, args, flops, smem=0):
    vmem, scalar = pl.BlockSpec(memory_space=pltpu.VMEM), pl.BlockSpec(memory_space=pltpu.SMEM)
    moved = sum(a.size * a.dtype.itemsize for a in args) + sum(4 * o[0] * o[1] for o in outs)
    single = len(outs) == 1
    shapes = [jax.ShapeDtypeStruct(o, f32) for o in outs]
    return pl.pallas_call(
        kernel,
        out_shape=shapes[0] if single else tuple(shapes),
        in_specs=[scalar] * smem + [vmem] * (len(args) - smem),
        out_specs=vmem if single else tuple([vmem] * len(outs)),
        scratch_shapes=[pltpu.VMEM(s, f32) for s in scratch],
        compiler_params=pltpu.CompilerParams(vmem_limit_bytes=24 << 20),
        cost_estimate=pl.CostEstimate(flops=flops, transcendentals=0, bytes_accessed=moved),
    )(*args)


def per_device(coupling, stiffness, loads, modes, joint_section, regime, participation):
    position, plane = lax.axis_index("sec"), lax.axis_index("mode")
    sections, groups = lax.axis_size("sec"), lax.axis_size("mode")
    size, columns = stiffness.shape[1], loads.shape[1]
    width = size // groups
    cells = len(upper(size))
    packed = (TILE * cells + columns * (size // TILE), TILE)
    square, stacked, thin_shape = (size, size), (size + columns, size), (columns, size)
    product = 6 * size**3

    def sent_to(value, where):
        pairs = []
        for s in range(sections):
            for m in range(groups):
                to = where(s, m)
                if to is not None and 0 <= to[0] < sections:
                    pairs.append((s * groups + m, to[0] * groups + to[1]))
        return lax.ppermute(value, AXES, pairs)

    def home(s):
        return s % 2 + 2 * ((s // 2 + s // 4) % 2) if groups == 4 else s % groups

    def parity(s, m):
        return (s - m) % min(2, groups) == 0

    block, thin, lower = stiffness[0], loads[0], coupling[0]

    matches = (jnp.arange(sections, dtype=jnp.int32)[:, None] == joint_section[None, :]).astype(f32)
    joint_regime = jnp.broadcast_to(regime[:, None], (regime.shape[0], BUCKET)).reshape(-1)
    joint_rate = jnp.zeros(joint_regime.shape, f32)
    for value_index, rate_value in enumerate(RATES):
        joint_rate = joint_rate + (joint_regime == value_index).astype(f32) * rate_value
    weights = participation.astype(f32)
    shares = jnp.dot(
        matches * joint_rate[None, :], weights * weights, precision=lax.Precision.HIGHEST
    )
    bits = sections.bit_length() - 1
    rounds = [[1]] + [[1 << b, 2 << b, 3 << b] if b + 1 < bits else [1 << b] for b in range(1, bits, 2)]

    def summed_over_sections(value):
        parts = [value]
        for steps in rounds:
            value = parts[0]
            for part in parts[1:]:
                value = value + part
            parts = [value] + [sent_to(value, lambda s, m, k=k: (s ^ k, m)) for k in steps]
        return parts

    shares = sum(summed_over_sections(shares))
    shares = lax.dynamic_slice_in_dim(shares, position, 1, 0)

    packed_down = call(pack_kernel, [packed], [], (block, thin), 0)
    packed_down = sent_to(packed_down, lambda s, m: (s + 1, m) if parity(s + 1, m) else None)

    def needs_lower(s, m):
        return m == home(s) or (s + 2 < sections and m == home(s + 2))

    lower_down = sent_to(lower, lambda s, m: (s + 1, m) if s >= 1 and needs_lower(s + 1, m) else None)
    lower_up = sent_to(lower, lambda s, m: (s - 1, m) if s >= 1 and m == home(s - 1) else None)
    up = call(own_kernel, [packed], [stacked, stacked], (block, thin, lower), 6 * product)
    up = sent_to(up, lambda s, m: (s - 1, m) if parity(s - 1, m) else None)
    through, full = call(receive_kernel, [square, stacked], [stacked, square], (packed_down, lower), 6 * product)
    sent, block, thin = call(fold_kernel, [packed, square, thin_shape], [], (block, thin, full, up), 0)

    packed_down = sent_to(sent, lambda s, m: (s + 2, m) if m == home(s + 2) else None)
    up = call(own_kernel, [packed], [stacked, stacked], (block, thin, through), 6 * product)
    up = sent_to(up, lambda s, m: (s - 2, m) if m == home(s - 2) else None)
    lower_down, shares = lax.optimization_barrier((lower_down, shares))
    lower = call(lower_kernel, [square], [], (through, lower_down), product)
    lower_down = sent_to(lower, lambda s, m: (s + 2, m) if s >= 2 and m == home(s + 2) else None)
    through, full = call(receive_kernel, [square, stacked], [stacked, square], (packed_down, lower), 6 * product)
    sent, block, thin = call(
        fold_above_kernel,
        [packed, square, thin_shape],
        [stacked, stacked, square],
        (up, lower_up, block, thin, full),
        2 * product,
    )

    packed_down = sent_to(sent, lambda s, m: (s + 4, home(s + 4)) if m == home(s) else None)
    inverse = call(whole_inverse_kernel, [square], [], (block,), 4 * product)
    lower, up = call(
        last_lower_kernel, [square, packed], [stacked, stacked], (through, lower_down, inverse, thin), 3 * product
    )
    up = sent_to(up, lambda s, m: (s - 4, home(s - 4)) if m == home(s) else None)
    inverse, thin_down = call(
        invert_kernel, [square, thin_shape], [square], (packed_down,), 4 * product
    )
    block, thin = call(
        last_receive_kernel, [square, thin_shape], [stacked], (inverse, thin_down, lower, block, thin), 2 * product
    )
    solved = call(solve_kernel, [thin_shape], [square, thin_shape], (block, thin, up), product)

    parts = [
        sent_to(solved, lambda s, m, k=k: (s, (m + k) % groups) if m == home(s) else None)
        for k in range(1, groups)
    ]
    homes = jnp.asarray([home(s) for s in range(sections)], jnp.int32)
    solved = jnp.where(homes[position] == plane, solved, 0.0)
    padded = (columns + 8, modes.shape[2])
    whole, payload = call(
        modal_kernel, [thin_shape, padded], [], (solved, *parts, modes[0], shares), product // 32
    )
    parts = summed_over_sections(payload)
    pieces = call(
        functools.partial(back_kernel_of, len(parts)),
        [(columns, width)] * groups,
        [thin_shape],
        (plane.reshape(1), *parts, modes[0]),
        product // 32,
        smem=1,
    )
    summed = pieces[0]
    for k in range(1, groups):
        summed = summed + sent_to(pieces[k], lambda s, m, k=k: (s, (m + k) % groups))
    own_columns = lax.dynamic_slice_in_dim(whole, plane * width, width, 1)
    return (own_columns[None], (own_columns - summed)[None])


def solution(mesh):
    in_specs = (
        P("sec", None, None),
        P("sec", None, None),
        P("sec", None, None),
        P("sec", None, "mode"),
        P("sec"),
        P("sec"),
        P("sec", "mode"),
    )
    out_specs = (P("sec", None, "mode"), P("sec", None, "mode"))
    return jax.shard_map(
        per_device, mesh=mesh, in_specs=in_specs, out_specs=out_specs, check_vma=False
    )
```

```python
import functools

import jax
import jax.numpy as jnp
from jax import lax
from jax.experimental import pallas as pl
from jax.experimental.pallas import tpu as pltpu
from jax.sharding import PartitionSpec as P

LEVELS = 3
BUCKET = 64
RATES = (0.2, 0.5, 1.0, 2.0)
AXES = ("sec", "mode")
TILE = 128
f32, bf16 = jnp.float32, jnp.bfloat16


def split(value):
    high = value.astype(bf16)
    return high, (value - high.astype(f32)).astype(bf16)


def dot(left, right):
    return jnp.dot(left, right, preferred_element_type=f32)


def dot_t(left, right):
    return lax.dot_general(left, right, (((1,), (1,)), ((), ())), preferred_element_type=f32)


def times(left, right, product=dot):
    return product(left[0], right[0]) + product(left[0], right[1]) + product(left[1], right[0])


def upper(size):
    count = size // TILE
    return [(a, b) for a in range(count) for b in range(a, count)]


def band(index):
    return slice(TILE * index, TILE * index + TILE)


def unpack(packed, block, thin):
    size = block.shape[0]
    cells = upper(size)
    for index, (a, b) in enumerate(cells):
        cell = packed[band(index), :]
        block[band(a), band(b)] = cell
        if a != b:
            block[band(b), band(a)] = cell.T
    rows = thin.shape[0]
    for c in range(size // TILE):
        start = TILE * len(cells) + rows * c
        thin[:, band(c)] = packed[start : start + rows, :]


def pack(packed, block, thin):
    size = block.shape[1]
    cells = upper(size)
    for index, (a, b) in enumerate(cells):
        packed[band(index), :] = block[band(a), band(b)]
    rows = thin.shape[0]
    for c in range(size // TILE):
        start = TILE * len(cells) + rows * c
        packed[start : start + rows, :] = thin[:, band(c)]


def scaled(block):
    size = block.shape[0]
    eye = lax.broadcasted_iota(jnp.int32, (size, size), 0) == lax.broadcasted_iota(
        jnp.int32, (size, size), 1
    )
    only = jnp.where(eye, block, 0.0)
    down = jnp.sum(only, axis=1, keepdims=True)
    along = jnp.sum(only, axis=0, keepdims=True)
    down = jnp.where(down == 0.0, 0.0, 1.0 / down)
    along = jnp.where(along == 0.0, 0.0, 1.0 / along)
    unit = jnp.where(eye, 1.0, 0.0)
    return unit, down, along, unit - down * block


def inverse_of(block):
    unit, down, along, first = scaled(block)
    one = split(first)
    second = times(one, one)
    two = split(second)
    third = dot(one[0], two[0])
    fourth = dot(two[0], two[0]).astype(bf16)
    series = unit + first + second + third
    series = series + dot(series.astype(bf16), fourth)
    return series * along


def schur(rows_and_thin, inverse, right, product):
    through = times(split(rows_and_thin), split(inverse))
    return through, times(split(through), split(right), product)


def pack_kernel(block, thin, packed, sems):
    size = block.shape[0]
    cells = upper(size)
    rows = thin.shape[0]
    pairs = [
        (block.at[band(a), band(b)], packed.at[band(index), :]) for index, (a, b) in enumerate(cells)
    ]
    for c in range(size // TILE):
        start = TILE * len(cells) + rows * c
        pairs.append((thin.at[:, band(c)], packed.at[start : start + rows, :]))
    copies = [pltpu.make_async_copy(src, dst, sems.at[k]) for k, (src, dst) in enumerate(pairs)]
    for copy in copies:
        copy.start()
    for copy in copies:
        copy.wait()


def folded(packed, block, thin, *others):
    size = block.shape[0]
    cells = upper(size)
    for index, (a, b) in enumerate(cells):
        value = block[band(a), band(b)]
        for other in others:
            same = other.shape == packed.shape
            value = value - (other[band(index), :] if same else other[band(a), band(b)])
        packed[band(index), :] = value
    rows = thin.shape[0]
    for c in range(size // TILE):
        start = TILE * len(cells) + rows * c
        value = thin[:, band(c)]
        for other in others:
            same = other.shape == packed.shape
            value = value - (other[start : start + rows, :] if same else other[size:, band(c)])
        packed[start : start + rows, :] = value


def own_kernel(block, thin, lower, packed, stack, out):
    size = block.shape[0]
    inverse = inverse_of(block[...])
    stack[0:size, :] = lower[...].T
    stack[size:, :] = thin[...]
    _, out[...] = schur(stack[...], inverse, lower[...], dot)
    pack(packed, out, out.at[size:, :])


def receive_kernel(packed, lower, through, full, stack, whole):
    size = lower.shape[0]
    unpack(packed, whole, stack.at[size:, :])
    inverse = inverse_of(whole[...])
    stack[0:size, :] = lower[...]
    half, full[...] = schur(stack[...], inverse, lower[...], dot_t)
    through[...] = half[0:size, :]


def fold_kernel(block, thin, full, above, packed, block_out, thin_out):
    folded(packed, block, thin, full, above)
    unpack(packed, block_out, thin_out)


def fold_above_kernel(packed_above, passed, block, thin, full, packed, block_out, thin_out, stack, out, whole):
    size = block.shape[0]
    unpack(packed_above, whole, stack.at[size:, :])
    right = split(passed[...])
    stack[0:size, :] = times(split(passed[...].T), split(whole[...]))
    stack[size:, :] = -stack[size:, :]
    out[...] = times(split(stack[...]), right)
    folded(packed, block, thin, full, out)
    unpack(packed, block_out, thin_out)


def whole_inverse_kernel(block, inverse):
    inverse[...] = inverse_of(block[...])


def invert_kernel(packed, inverse, thin, block):
    unpack(packed, block, thin)
    inverse[...] = inverse_of(block[...])


def lower_kernel(through, passed, after, lower):
    lower[...] = -times(split(through[...]), split(passed[...]))


def last_lower_kernel(through, passed, inverse, thin, lower, packed, stack, out):
    size = inverse.shape[0]
    value = -times(split(through[...]), split(passed[...]))
    lower[...] = value
    stack[0:size, :] = value.T
    stack[size:, :] = thin[...]
    _, out[...] = schur(stack[...], inverse[...], value, dot)
    pack(packed, out, out.at[size:, :])


def last_receive_kernel(inverse, thin_passed, lower, block, thin, block_out, thin_out, stack):
    size = block.shape[0]
    stack[0:size, :] = lower[...]
    stack[size:, :] = thin_passed[...]
    _, full = schur(stack[...], inverse[...], lower[...], dot_t)
    block_out[...] = block[...] - full[0:size, :]
    thin_out[...] = thin[...] - full[size:, :]


def solve_kernel(block, thin, above, solution, whole, own):
    unpack(above, whole, own)
    value = block[...] - whole[...]
    unit, _, along, _ = scaled(value)
    high, low = split(unit - value * along)
    rows = thin.shape[0]
    now = (thin[...] - own[...]) * along
    for power in (1, 2, 4):
        moved = now
        for _ in range(power):
            top, rest = split(moved)
            both = dot(jnp.concatenate([top, rest], axis=0), high)
            moved = both[0:rows, :] + both[rows:, :] + dot(top, low)
        now = now + moved
    solution[...] = now


def modal_kernel(a, b, c, d, modes, shares, whole, payload):
    value = a[...] + b[...] + c[...] + d[...]
    whole[...] = value
    amplitude = jnp.sqrt(jnp.sum(value * value, keepdims=True) / value.size + 1e-06)
    rows = value.shape[0]
    payload[...] = jnp.zeros_like(payload)
    payload[0:rows, :] = dot(value.astype(bf16), modes[...])
    payload[rows : rows + 1, :] = shares[...] * (amplitude / (1.0 + amplitude))


def back_kernel_of(count, place, *refs):
    parts, modes, pieces, scratch = refs[:count], refs[count], refs[count + 1 : -1], refs[-1]
    total = parts[0][...]
    for part in parts[1:]:
        total = total + part[...]
    rows = scratch.shape[0]
    damping = total[rows : rows + 1, :]
    removed = (total[0:rows, :] * (damping / (1.0 + damping))).astype(bf16)
    scratch[...] = dot_t(removed, modes[...])
    width = pieces[0].shape[1]
    for k, piece in enumerate(pieces):
        start = lax.rem(place[0] + k, len(pieces)) * width
        piece[...] = scratch[:, pl.ds(pl.multiple_of(start, width), width)]


def packed_from_hbm(block, thin, packed):
    cells = len(upper(block.shape[0])) + block.shape[0] // TILE
    return pl.pallas_call(
        pack_kernel,
        out_shape=jax.ShapeDtypeStruct(packed, f32),
        in_specs=[pl.BlockSpec(memory_space=pl.ANY)] * 2,
        out_specs=pl.BlockSpec(memory_space=pltpu.VMEM),
        scratch_shapes=[pltpu.SemaphoreType.DMA((cells,))],
    )(block, thin)


def call(kernel, outs, scratch, args, flops, smem=0, after=0):
    vmem, scalar = pl.BlockSpec(memory_space=pltpu.VMEM), pl.BlockSpec(memory_space=pltpu.SMEM)
    single = len(outs) == 1
    shapes = [jax.ShapeDtypeStruct(o, f32) for o in outs]
    return pl.pallas_call(
        kernel,
        out_shape=shapes[0] if single else tuple(shapes),
        in_specs=[scalar] * smem
        + [vmem] * (len(args) - smem - after)
        + [pl.BlockSpec(memory_space=pl.ANY)] * after,
        out_specs=vmem if single else tuple([vmem] * len(outs)),
        scratch_shapes=[pltpu.VMEM(s, f32) for s in scratch],
        compiler_params=pltpu.CompilerParams(vmem_limit_bytes=20 << 20),
        cost_estimate=pl.CostEstimate(flops=int(flops), transcendentals=0, bytes_accessed=1024),
    )(*args)


def per_device(coupling, stiffness, loads, modes, joint_section, regime, participation):
    position, plane = lax.axis_index("sec"), lax.axis_index("mode")
    sections, groups = lax.axis_size("sec"), lax.axis_size("mode")
    assert groups == 4 and LEVELS == 3
    size, columns = stiffness.shape[1], loads.shape[1]
    width = size // groups
    cells = len(upper(size))
    packed = (TILE * cells + columns * (size // TILE), TILE)
    square, stacked, thin_shape = (size, size), (size + columns, size), (columns, size)
    product = 0.05 * 6 * size**3
    long = 1.0 * 6 * size**3

    def sent_to(value, where):
        pairs = []
        for s in range(sections):
            for m in range(groups):
                to = where(s, m)
                if to is not None and 0 <= to[0] < sections:
                    pairs.append((s * groups + m, to[0] * groups + to[1]))
        return lax.ppermute(value, AXES, pairs)

    def home(s):
        return 2 * (s % 2) + (s // 2 + s // 4) % 2

    def parity(s, m):
        return m // 2 == s % 2

    block, thin, lower = stiffness[0], loads[0], coupling[0]

    matches = (jnp.arange(sections, dtype=jnp.int32)[:, None] == joint_section[None, :]).astype(f32)
    joint_regime = jnp.broadcast_to(regime[:, None], (regime.shape[0], BUCKET)).reshape(-1)
    joint_rate = jnp.zeros(joint_regime.shape, f32)
    for value_index, rate_value in enumerate(RATES):
        joint_rate = joint_rate + (joint_regime == value_index).astype(f32) * rate_value
    weights = participation.astype(f32)
    shares = jnp.dot(
        matches * joint_rate[None, :], weights * weights, precision=lax.Precision.HIGHEST
    )
    bits = sections.bit_length() - 1
    rounds = [[1]] + [[1 << b, 2 << b, 3 << b] if b + 1 < bits else [1 << b] for b in range(1, bits, 2)]

    def summed_over_sections(value):
        parts = [value]
        for steps in rounds:
            value = parts[0]
            for part in parts[1:]:
                value = value + part
            parts = [value] + [sent_to(value, lambda s, m, k=k: (s ^ k, m)) for k in steps]
        return parts

    shares = sum(summed_over_sections(shares))
    shares = lax.dynamic_slice_in_dim(shares, position, 1, 0)

    packed_down = packed_from_hbm(block, thin, packed)
    lower_sent, packed_down = lax.optimization_barrier((lower, packed_down))
    packed_down = sent_to(packed_down, lambda s, m: (s + 1, m) if parity(s + 1, m) else None)

    def needs_lower(s, m):
        return m == home(s) or (s + 2 < sections and m == home(s + 2))

    lower_down = sent_to(lower_sent, lambda s, m: (s + 1, m) if s >= 1 and needs_lower(s + 1, m) else None)
    lower_up = sent_to(lower_sent, lambda s, m: (s - 1, m) if s >= 1 and m == home(s - 1) else None)
    up = call(own_kernel, [packed], [stacked, stacked], (block, thin, lower), 6 * product)
    up = sent_to(up, lambda s, m: (s - 1, m) if parity(s - 1, m) else None)
    through, full = call(receive_kernel, [square, stacked], [stacked, square], (packed_down, lower), 6 * long)
    sent, block, thin = call(fold_kernel, [packed, square, thin_shape], [], (block, thin, full, up), 0)

    packed_down = sent_to(sent, lambda s, m: (s + 2, m) if m == home(s + 2) else None)
    bracket = call(own_kernel, [packed], [stacked, stacked], (block, thin, through), 6 * product)
    up = sent_to(bracket, lambda s, m: (s - 2, m) if m == home(s - 2) else None)
    lower = call(lower_kernel, [square], [], (through, lower_down, bracket), product, after=1)
    lower_down = sent_to(lower, lambda s, m: (s + 2, m) if s >= 2 and m == home(s + 2) else None)
    packed_down, shares = lax.optimization_barrier((packed_down, shares))
    through, full = call(receive_kernel, [square, stacked], [stacked, square], (packed_down, lower), 6 * long)
    sent, block, thin = call(
        fold_above_kernel,
        [packed, square, thin_shape],
        [stacked, stacked, square],
        (up, lower_up, block, thin, full),
        2 * long,
    )

    packed_down = sent_to(sent, lambda s, m: (s + 4, home(s + 4)) if m == home(s) else None)
    inverse = call(whole_inverse_kernel, [square], [], (block,), 4 * long)
    lower, up = call(
        last_lower_kernel, [square, packed], [stacked, stacked], (through, lower_down, inverse, thin), 3 * product
    )
    up = sent_to(up, lambda s, m: (s - 4, home(s - 4)) if m == home(s) else None)
    inverse, thin_down = call(
        invert_kernel, [square, thin_shape], [square], (packed_down,), 4 * product
    )
    block, thin = call(
        last_receive_kernel, [square, thin_shape], [stacked], (inverse, thin_down, lower, block, thin), 2 * product
    )
    solved = call(solve_kernel, [thin_shape], [square, thin_shape], (block, thin, up), product)

    parts = [
        sent_to(solved, lambda s, m, k=k: (s, (m + k) % groups) if m == home(s) else None)
        for k in range(1, groups)
    ]
    homes = jnp.asarray([home(s) for s in range(sections)], jnp.int32)
    solved = jnp.where(homes[position] == plane, solved, 0.0)
    padded = (columns + 8, modes.shape[2])
    whole, payload = call(
        modal_kernel, [thin_shape, padded], [], (solved, *parts, modes[0], shares), product // 32
    )
    parts = summed_over_sections(payload)
    pieces = call(
        functools.partial(back_kernel_of, len(parts)),
        [(columns, width)] * groups,
        [thin_shape],
        (plane.reshape(1), *parts, modes[0]),
        product // 32,
        smem=1,
    )
    summed = pieces[0]
    for k in range(1, groups):
        summed = summed + sent_to(pieces[k], lambda s, m, k=k: (s, (m + k) % groups))
    own_columns = lax.dynamic_slice_in_dim(whole, plane * width, width, 1)
    return (own_columns[None], (own_columns - summed)[None])


def solution(mesh):
    in_specs = (
        P("sec", None, None),
        P("sec", None, None),
        P("sec", None, None),
        P("sec", None, "mode"),
        P("sec"),
        P("sec"),
        P("sec", "mode"),
    )
    out_specs = (P("sec", None, "mode"), P("sec", None, "mode"))
    return jax.shard_map(
        per_device, mesh=mesh, in_specs=in_specs, out_specs=out_specs, check_vma=False
    )
```

```python
import functools

import jax
import jax.numpy as jnp
from jax import lax
from jax.experimental import pallas as pl
from jax.experimental.pallas import tpu as pltpu
from jax.sharding import PartitionSpec as P

LEVELS = 3
BUCKET = 64
RATES = (0.2, 0.5, 1.0, 2.0)
AXES = ("sec", "mode")
TILE = 128
f32, bf16 = jnp.float32, jnp.bfloat16


def split(value):
    high = value.astype(bf16)
    return high, (value - high.astype(f32)).astype(bf16)


def dot(left, right):
    return jnp.dot(left, right, preferred_element_type=f32)


def dot_t(left, right):
    return lax.dot_general(left, right, (((1,), (1,)), ((), ())), preferred_element_type=f32)


def times(left, right, product=dot):
    return product(left[0], right[0]) + product(left[0], right[1]) + product(left[1], right[0])


def upper(size):
    count = size // TILE
    return [(a, b) for a in range(count) for b in range(a, count)]


def band(index):
    return slice(TILE * index, TILE * index + TILE)


def unpack(packed, block, thin):
    size = block.shape[0]
    cells = upper(size)
    for index, (a, b) in enumerate(cells):
        cell = packed[band(index), :]
        block[band(a), band(b)] = cell
        if a != b:
            block[band(b), band(a)] = cell.T
    rows = thin.shape[0]
    for c in range(size // TILE):
        start = TILE * len(cells) + rows * c
        thin[:, band(c)] = packed[start : start + rows, :]


def pack(packed, block, thin):
    size = block.shape[1]
    cells = upper(size)
    for index, (a, b) in enumerate(cells):
        packed[band(index), :] = block[band(a), band(b)]
    rows = thin.shape[0]
    for c in range(size // TILE):
        start = TILE * len(cells) + rows * c
        packed[start : start + rows, :] = thin[:, band(c)]


def scaled(block):
    size = block.shape[0]
    eye = lax.broadcasted_iota(jnp.int32, (size, size), 0) == lax.broadcasted_iota(
        jnp.int32, (size, size), 1
    )
    only = jnp.where(eye, block, 0.0)
    down = jnp.sum(only, axis=1, keepdims=True)
    along = jnp.sum(only, axis=0, keepdims=True)
    down = jnp.where(down == 0.0, 0.0, 1.0 / down)
    along = jnp.where(along == 0.0, 0.0, 1.0 / along)
    unit = jnp.where(eye, 1.0, 0.0)
    return unit, down, along, unit - down * block


def inverse_of(block):
    unit, down, along, first = scaled(block)
    one = split(first)
    second = times(one, one)
    two = split(second)
    third = dot(one[0], two[0])
    fourth = dot(two[0], two[0]).astype(bf16)
    series = unit + first + second + third
    series = series + dot(series.astype(bf16), fourth)
    return series * along


def schur(rows_and_thin, inverse, right, product):
    through = times(split(rows_and_thin), split(inverse))
    return through, times(split(through), split(right), product)


def pack_kernel(block, thin, packed, sems):
    size = block.shape[0]
    cells = upper(size)
    rows = thin.shape[0]
    pairs = [
        (block.at[band(a), band(b)], packed.at[band(index), :]) for index, (a, b) in enumerate(cells)
    ]
    for c in range(size // TILE):
        start = TILE * len(cells) + rows * c
        pairs.append((thin.at[:, band(c)], packed.at[start : start + rows, :]))
    copies = [pltpu.make_async_copy(src, dst, sems.at[k]) for k, (src, dst) in enumerate(pairs)]
    for copy in copies:
        copy.start()
    for copy in copies:
        copy.wait()


def folded(packed, block, thin, *others):
    size = block.shape[0]
    cells = upper(size)
    for index, (a, b) in enumerate(cells):
        value = block[band(a), band(b)]
        for other in others:
            same = other.shape == packed.shape
            value = value - (other[band(index), :] if same else other[band(a), band(b)])
        packed[band(index), :] = value
    rows = thin.shape[0]
    for c in range(size // TILE):
        start = TILE * len(cells) + rows * c
        value = thin[:, band(c)]
        for other in others:
            same = other.shape == packed.shape
            value = value - (other[start : start + rows, :] if same else other[size:, band(c)])
        packed[start : start + rows, :] = value


def first_own_kernel(block, thin, lower_hbm, packed, stack, out, lower, sem):
    copy = pltpu.make_async_copy(lower_hbm, lower, sem)
    copy.start()
    own_kernel(block, thin, lower, packed, stack, out, copy)


def own_kernel(block, thin, lower, packed, stack, out, copy=None):
    size = block.shape[0]
    inverse = inverse_of(block[...])
    if copy is not None:
        copy.wait()
    stack[0:size, :] = lower[...].T
    stack[size:, :] = thin[...]
    _, out[...] = schur(stack[...], inverse, lower[...], dot)
    pack(packed, out, out.at[size:, :])


def bracket_kernel(block, thin, lower, packed, done, stack, out):
    own_kernel(block, thin, lower, packed, stack, out)
    done[...] = jnp.zeros_like(done)


def first_receive_kernel(packed, lower_hbm, through, full, stack, whole, lower, sem):
    copy = pltpu.make_async_copy(lower_hbm, lower, sem)
    copy.start()
    receive_kernel(packed, lower, through, full, stack, whole, copy)


def receive_kernel(packed, lower, through, full, stack, whole, copy=None):
    size = lower.shape[0]
    unpack(packed, whole, stack.at[size:, :])
    inverse = inverse_of(whole[...])
    if copy is not None:
        copy.wait()
    stack[0:size, :] = lower[...]
    half, full[...] = schur(stack[...], inverse, lower[...], dot_t)
    through[...] = half[0:size, :]


def fold_kernel(block, thin, full, above, packed, block_out, thin_out):
    folded(packed, block, thin, full, above)
    unpack(packed, block_out, thin_out)


def fold_above_kernel(packed_above, passed, block, thin, full, packed, block_out, thin_out, stack, out, whole):
    size = block.shape[0]
    unpack(packed_above, whole, stack.at[size:, :])
    right = split(passed[...])
    stack[0:size, :] = times(split(passed[...].T), split(whole[...]))
    stack[size:, :] = -stack[size:, :]
    out[...] = times(split(stack[...]), right)
    folded(packed, block, thin, full, out)
    unpack(packed, block_out, thin_out)


def whole_inverse_kernel(needed, block, inverse):
    @pl.when(needed())
    def _():
        inverse[...] = inverse_of(block[...])


def lower_kernel(through, passed, after, lower):
    lower[...] = -times(split(through[...]), split(passed[...]))


def last_lower_kernel(needed, through, passed, inverse, thin, lower, packed, stack, out):
    size = inverse.shape[0]

    @pl.when(needed())
    def _():
        value = -times(split(through[...]), split(passed[...]))
        lower[...] = value
        stack[0:size, :] = value.T
        stack[size:, :] = thin[...]
        _, out[...] = schur(stack[...], inverse[...], value, dot)
        pack(packed, out, out.at[size:, :])


def last_receive_kernel(needed, packed, lower, block, thin, block_out, thin_out, stack, whole):
    size = block.shape[0]

    @pl.when(needed())
    def _():
        unpack(packed, whole, stack.at[size:, :])
        inverse = inverse_of(whole[...])
        stack[0:size, :] = lower[...]
        _, full = schur(stack[...], inverse, lower[...], dot_t)
        block_out[...] = block[...] - full[0:size, :]
        thin_out[...] = thin[...] - full[size:, :]

    @pl.when(jnp.logical_not(needed()))
    def _():
        block_out[...] = block[...]
        thin_out[...] = thin[...]


def solve_kernel(block, thin, above, solution, whole, own):
    unpack(above, whole, own)
    value = block[...] - whole[...]
    unit, _, along, _ = scaled(value)
    high, low = split(unit - value * along)
    rows = thin.shape[0]
    now = (thin[...] - own[...]) * along
    for power in (1, 2, 4):
        moved = now
        for _ in range(power):
            top, rest = split(moved)
            both = dot(jnp.concatenate([top, rest], axis=0), high)
            moved = both[0:rows, :] + both[rows:, :] + dot(top, low)
        now = now + moved
    solution[...] = now


def shares_kernel(regime, joints, participation, shares):
    sections, count = shares.shape[0], joints.shape[1]
    bucket = lax.broadcasted_iota(jnp.int32, (1, count), 1) // BUCKET
    rate = jnp.zeros((1, count), f32)
    for b in range(count // BUCKET):
        value = jnp.float32(0.0)
        for index, known in enumerate(RATES):
            value = jnp.where(regime[b] == index, jnp.float32(known), value)
        rate = jnp.where(bucket == b, value, rate)
    section = lax.broadcasted_iota(jnp.int32, (sections, count), 0)
    weights = jnp.where(section == joints[...], rate, 0.0)
    squares = participation[...].astype(f32)
    shares[...] = times(split(weights), split(squares * squares))


def modal_kernel(home, a, b, c, d, modes, shares, whole, payload):
    position, plane = lax.axis_index("sec"), lax.axis_index("mode")
    own = jnp.where(home(position) == plane, a[...], 0.0)
    value = own + b[...] + c[...] + d[...]
    whole[...] = value
    amplitude = jnp.sqrt(jnp.sum(value * value, keepdims=True) / value.size + 1e-06)
    rows, sections = value.shape[0], shares.shape[0]
    payload[0:rows, :] = dot(value.astype(bf16), modes[...])
    payload[rows : rows + sections, :] = shares[...]
    mine = lax.broadcasted_iota(jnp.int32, shares.shape, 0) == position
    payload[rows + sections :, :] = jnp.where(mine, amplitude / (1.0 + amplitude), 0.0)


def back_kernel_of(count, *refs):
    plane = lax.axis_index("mode")
    parts, modes, pieces, scratch = refs[:count], refs[count], refs[count + 1 : -1], refs[-1]
    total = parts[0][...]
    for part in parts[1:]:
        total = total + part[...]
    rows = scratch.shape[0]
    sections = (total.shape[0] - rows) // 2
    parts = total[rows : rows + sections, :] * total[rows + sections :, :]
    damping = jnp.sum(parts, axis=0, keepdims=True)
    removed = (total[0:rows, :] * (damping / (1.0 + damping))).astype(bf16)
    scratch[...] = dot_t(removed, modes[...])
    width = pieces[0].shape[1]
    for k, piece in enumerate(pieces):
        start = lax.rem(plane + k, len(pieces)) * width
        piece[...] = scratch[:, pl.ds(pl.multiple_of(start, width), width)]


def packed_from_hbm(block, thin, packed):
    cells = len(upper(block.shape[0])) + block.shape[0] // TILE
    return pl.pallas_call(
        pack_kernel,
        out_shape=pltpu.VMEM(packed, f32),
        in_specs=[pl.BlockSpec(memory_space=pl.ANY)] * 2,
        out_specs=pl.BlockSpec(memory_space=pltpu.VMEM),
        scratch_shapes=[pltpu.SemaphoreType.DMA((cells,))],
    )(block, thin)


def call(kernel, outs, scratch, args, flops, smem=0, hbm=0):
    vmem, scalar = pl.BlockSpec(memory_space=pltpu.VMEM), pl.BlockSpec(memory_space=pltpu.SMEM)
    moved = sum(a.size * a.dtype.itemsize for a in args) + sum(4 * o[0] * o[1] for o in outs)
    single = len(outs) == 1
    shapes = [jax.ShapeDtypeStruct(o, f32) for o in outs]
    return pl.pallas_call(
        kernel,
        out_shape=shapes[0] if single else tuple(shapes),
        in_specs=[scalar] * smem
        + [vmem] * (len(args) - smem - hbm)
        + [pl.BlockSpec(memory_space=pl.ANY)] * hbm,
        out_specs=vmem if single else tuple([vmem] * len(outs)),
        scratch_shapes=[pltpu.VMEM(s, f32) for s in scratch] + [pltpu.SemaphoreType.DMA] * hbm,
        compiler_params=pltpu.CompilerParams(vmem_limit_bytes=14 << 20),
        cost_estimate=pl.CostEstimate(flops=int(flops), transcendentals=0, bytes_accessed=moved),
    )(*args)


def per_device(coupling, stiffness, loads, modes, joint_section, regime, participation):
    sections, groups = lax.axis_size("sec"), lax.axis_size("mode")
    assert groups == 4 and LEVELS == 3
    size, columns = stiffness.shape[1], loads.shape[1]
    width = size // groups
    cells = len(upper(size))
    packed = (TILE * cells + columns * (size // TILE), TILE)
    square, stacked, thin_shape = (size, size), (size + columns, size), (columns, size)
    product = 0.1 * 6 * size**3
    long = 1.0 * 6 * size**3

    def sent_to(value, where):
        pairs = []
        for s in range(sections):
            for m in range(groups):
                to = where(s, m)
                if to is not None and 0 <= to[0] < sections:
                    pairs.append((s * groups + m, to[0] * groups + to[1]))
        return lax.ppermute(value, AXES, pairs)

    def home(s):
        return 2 * (s % 2) + (s // 2 + s // 4) % 2

    def parity(s, m):
        return m // 2 == s % 2

    block, thin, lower = stiffness[0], loads[0], coupling[0]

    shares = call(
        shares_kernel,
        [(sections, participation.shape[1])],
        [],
        (regime, joint_section[None, :], participation),
        product // 32,
        smem=1,
    )
    bits = sections.bit_length() - 1
    rounds = [[1]] + [[1 << b, 2 << b, 3 << b] if b + 1 < bits else [1 << b] for b in range(1, bits, 2)]

    def summed_over_sections(value):
        parts = [value]
        for steps in rounds:
            value = parts[0]
            for part in parts[1:]:
                value = value + part
            parts = [value] + [sent_to(value, lambda s, m, k=k: (s ^ k, m)) for k in steps]
        return parts

    packed_down = packed_from_hbm(block, thin, packed)
    lower_sent, packed_down = lax.optimization_barrier((lower, packed_down))
    packed_down = sent_to(packed_down, lambda s, m: (s + 1, m) if parity(s + 1, m) else None)

    def needs_lower(s, m):
        return m == home(s) or (s + 2 < sections and m == home(s + 2))

    lower_down = sent_to(lower_sent, lambda s, m: (s + 1, m) if s >= 1 and needs_lower(s + 1, m) else None)
    lower_up = sent_to(lower_sent, lambda s, m: (s - 1, m) if s >= 1 and m == home(s - 1) else None)
    up = call(
        first_own_kernel, [packed], [stacked, stacked, square], (block, thin, lower), 6 * product, hbm=1
    )
    up = sent_to(up, lambda s, m: (s - 1, m) if parity(s - 1, m) else None)
    through, full = call(
        first_receive_kernel, [square, stacked], [stacked, square, square], (packed_down, lower), 6 * long, hbm=1
    )
    sent, block, thin = call(fold_kernel, [packed, square, thin_shape], [], (block, thin, full, up), 0)

    packed_down = sent_to(sent, lambda s, m: (s + 2, m) if m == home(s + 2) else None)
    up, done = call(
        bracket_kernel, [packed, (8, TILE)], [stacked, stacked], (block, thin, through), 6 * product
    )
    up = sent_to(up, lambda s, m: (s - 2, m) if m == home(s - 2) else None)
    lower = call(lower_kernel, [square], [], (through, lower_down, done), product)
    lower_down = sent_to(lower, lambda s, m: (s + 2, m) if s >= 2 and m == home(s + 2) else None)
    packed_down, lower_up, shares = lax.optimization_barrier((packed_down, lower_up, shares))
    through, full = call(receive_kernel, [square, stacked], [stacked, square], (packed_down, lower), 60 * product)
    sent, block, thin = call(
        fold_above_kernel,
        [packed, square, thin_shape],
        [stacked, stacked, square],
        (up, lower_up, block, thin, full),
        2 * long,
    )

    sent, lower_down = lax.optimization_barrier((sent, lower_down))
    packed_down = sent_to(sent, lambda s, m: (s + 4, home(s + 4)) if m == home(s) else None)
    has_before = lambda: lax.axis_index("sec") >= 4
    inverse = call(functools.partial(whole_inverse_kernel, has_before), [square], [], (block,), 4 * long)
    lower, up = call(
        functools.partial(last_lower_kernel, has_before), [square, packed], [stacked, stacked], (through, lower_down, inverse, thin), 3 * product
    )
    up = sent_to(up, lambda s, m: (s - 4, home(s - 4)) if m == home(s) else None)
    block, thin = call(
        functools.partial(last_receive_kernel, has_before),
        [square, thin_shape],
        [stacked, square],
        (packed_down, lower, block, thin),
        6 * product,
    )
    solved = call(solve_kernel, [thin_shape], [square, thin_shape], (block, thin, up), product)

    parts = [
        sent_to(solved, lambda s, m, k=k: (s, (m + k) % groups) if m == home(s) else None)
        for k in range(1, groups)
    ]
    whole, payload = call(
        functools.partial(modal_kernel, home),
        [thin_shape, (columns + 2 * sections, modes.shape[2])],
        [],
        (solved, *parts, modes[0], shares),
        product // 32,
    )
    parts = summed_over_sections(payload)
    pieces = call(
        functools.partial(back_kernel_of, len(parts)),
        [(columns, width)] * groups,
        [thin_shape],
        (*parts, modes[0]),
        product // 32,
    )
    summed = pieces[0]
    for k in range(1, groups):
        summed = summed + sent_to(pieces[k], lambda s, m, k=k: (s, (m + k) % groups))
    own_columns = lax.dynamic_slice_in_dim(whole, lax.axis_index("mode") * width, width, 1)
    return (own_columns[None], (own_columns - summed)[None])


def solution(mesh):
    in_specs = (
        P("sec", None, None),
        P("sec", None, None),
        P("sec", None, None),
        P("sec", None, "mode"),
        P("sec"),
        P("sec"),
        P("sec", "mode"),
    )
    out_specs = (P("sec", None, "mode"), P("sec", None, "mode"))
    return jax.shard_map(
        per_device, mesh=mesh, in_specs=in_specs, out_specs=out_specs, check_vma=False
    )
```

```python
import functools

import jax
import jax.numpy as jnp
from jax import lax
from jax.experimental import pallas as pl
from jax.experimental.pallas import tpu as pltpu
from jax.sharding import PartitionSpec as P

LEVELS = 3
BUCKET = 64
RATES = (0.2, 0.5, 1.0, 2.0)
AXES = ("sec", "mode")
TILE = 128
f32, bf16 = jnp.float32, jnp.bfloat16


def split(value):
    high = value.astype(bf16)
    return high, (value - high.astype(f32)).astype(bf16)


def dot(left, right):
    return jnp.dot(left, right, preferred_element_type=f32)


def dot_t(left, right):
    return lax.dot_general(left, right, (((1,), (1,)), ((), ())), preferred_element_type=f32)


def times(left, right, product=dot):
    return product(left[0], right[0]) + product(left[0], right[1]) + product(left[1], right[0])


def upper(size):
    count = size // TILE
    return [(a, b) for a in range(count) for b in range(a, count)]


def band(index):
    return slice(TILE * index, TILE * index + TILE)


def unpack(packed, block, thin):
    size = block.shape[0]
    cells = upper(size)
    for index, (a, b) in enumerate(cells):
        cell = packed[band(index), :]
        block[band(a), band(b)] = cell
        if a != b:
            block[band(b), band(a)] = cell.T
    rows = thin.shape[0]
    for c in range(size // TILE):
        start = TILE * len(cells) + rows * c
        thin[:, band(c)] = packed[start : start + rows, :]


def pack(packed, block, thin):
    size = block.shape[1]
    cells = upper(size)
    for index, (a, b) in enumerate(cells):
        packed[band(index), :] = block[band(a), band(b)]
    rows = thin.shape[0]
    for c in range(size // TILE):
        start = TILE * len(cells) + rows * c
        packed[start : start + rows, :] = thin[:, band(c)]


def scaled(block):
    size = block.shape[0]
    eye = lax.broadcasted_iota(jnp.int32, (size, size), 0) == lax.broadcasted_iota(
        jnp.int32, (size, size), 1
    )
    only = jnp.where(eye, block, 0.0)
    down = jnp.sum(only, axis=1, keepdims=True)
    along = jnp.sum(only, axis=0, keepdims=True)
    down = jnp.where(down == 0.0, 0.0, 1.0 / down)
    along = jnp.where(along == 0.0, 0.0, 1.0 / along)
    unit = jnp.where(eye, 1.0, 0.0)
    return unit, down, along, unit - down * block


def inverse_of(block):
    unit, down, along, first = scaled(block)
    one = split(first)
    second = times(one, one)
    two = split(second)
    third = dot(one[0], two[0])
    fourth = dot(two[0], two[0]).astype(bf16)
    series = unit + first + second + third
    series = series + dot(series.astype(bf16), fourth)
    return series * along


def schur(rows_and_thin, inverse, right, product):
    through = times(split(rows_and_thin), split(inverse))
    return through, times(split(through), split(right), product)


def pack_kernel(block, thin, packed, sems):
    size = block.shape[0]
    cells = upper(size)
    rows = thin.shape[0]
    pairs = [
        (block.at[band(a), band(b)], packed.at[band(index), :]) for index, (a, b) in enumerate(cells)
    ]
    for c in range(size // TILE):
        start = TILE * len(cells) + rows * c
        pairs.append((thin.at[:, band(c)], packed.at[start : start + rows, :]))
    copies = [pltpu.make_async_copy(src, dst, sems.at[k]) for k, (src, dst) in enumerate(pairs)]
    for copy in copies:
        copy.start()
    for copy in copies:
        copy.wait()


def folded(packed, block, thin, *others):
    size = block.shape[0]
    cells = upper(size)
    for index, (a, b) in enumerate(cells):
        value = block[band(a), band(b)]
        for other in others:
            same = other.shape == packed.shape
            value = value - (other[band(index), :] if same else other[band(a), band(b)])
        packed[band(index), :] = value
    rows = thin.shape[0]
    for c in range(size // TILE):
        start = TILE * len(cells) + rows * c
        value = thin[:, band(c)]
        for other in others:
            same = other.shape == packed.shape
            value = value - (other[start : start + rows, :] if same else other[size:, band(c)])
        packed[start : start + rows, :] = value


def first_own_kernel(block, thin, lower_hbm, packed, stack, out, lower, sem):
    copy = pltpu.make_async_copy(lower_hbm, lower, sem)
    copy.start()
    own_kernel(block, thin, lower, packed, stack, out, copy)


def own_kernel(block, thin, lower, packed, stack, out, copy=None):
    size = block.shape[0]
    inverse = inverse_of(block[...])
    if copy is not None:
        copy.wait()
    stack[0:size, :] = lower[...].T
    stack[size:, :] = thin[...]
    _, out[...] = schur(stack[...], inverse, lower[...], dot)
    pack(packed, out, out.at[size:, :])


def bracket_kernel(block, thin, lower, packed, done, stack, out):
    own_kernel(block, thin, lower, packed, stack, out)
    done[...] = jnp.zeros_like(done)


def first_receive_kernel(packed, lower_hbm, through, full, stack, whole, lower, sem):
    copy = pltpu.make_async_copy(lower_hbm, lower, sem)
    copy.start()
    receive_kernel(packed, lower, through, full, stack, whole, copy)


def receive_kernel(packed, lower, through, full, stack, whole, copy=None):
    size = lower.shape[0]
    unpack(packed, whole, stack.at[size:, :])
    inverse = inverse_of(whole[...])
    if copy is not None:
        copy.wait()
    stack[0:size, :] = lower[...]
    half, full[...] = schur(stack[...], inverse, lower[...], dot_t)
    through[...] = half[0:size, :]


def fold_kernel(block, thin, full, above, packed, block_out, thin_out):
    folded(packed, block, thin, full, above)
    unpack(packed, block_out, thin_out)


def fold_above_kernel(packed_above, passed, block, thin, full, packed, block_out, thin_out, stack, out, whole):
    size = block.shape[0]
    unpack(packed_above, whole, stack.at[size:, :])
    right = split(passed[...])
    stack[0:size, :] = times(split(passed[...].T), split(whole[...]))
    stack[size:, :] = -stack[size:, :]
    out[...] = times(split(stack[...]), right)
    folded(packed, block, thin, full, out)
    unpack(packed, block_out, thin_out)


def whole_inverse_kernel(needed, block, inverse):
    @pl.when(needed())
    def _():
        inverse[...] = inverse_of(block[...])


def lower_kernel(through, passed, after, lower):
    lower[...] = -times(split(through[...]), split(passed[...]))


def last_lower_kernel(needed, through, passed, inverse, thin, lower, packed, stack, out):
    size = inverse.shape[0]

    @pl.when(needed())
    def _():
        value = -times(split(through[...]), split(passed[...]))
        lower[...] = value
        stack[0:size, :] = value.T
        stack[size:, :] = thin[...]
        _, out[...] = schur(stack[...], inverse[...], value, dot)
        pack(packed, out, out.at[size:, :])


def last_receive_kernel(needed, packed, lower, block, thin, block_out, thin_out, stack, whole):
    size = block.shape[0]

    @pl.when(needed())
    def _():
        unpack(packed, whole, stack.at[size:, :])
        inverse = inverse_of(whole[...])
        stack[0:size, :] = lower[...]
        _, full = schur(stack[...], inverse, lower[...], dot_t)
        block_out[...] = block[...] - full[0:size, :]
        thin_out[...] = thin[...] - full[size:, :]

    @pl.when(jnp.logical_not(needed()))
    def _():
        block_out[...] = block[...]
        thin_out[...] = thin[...]


def solve_kernel(block, thin, above, solution, whole, own):
    unpack(above, whole, own)
    value = block[...] - whole[...]
    unit, _, along, _ = scaled(value)
    high, low = split(unit - value * along)
    rows = thin.shape[0]
    now = (thin[...] - own[...]) * along
    for power in (1, 2, 4):
        moved = now
        for _ in range(power):
            top, rest = split(moved)
            both = dot(jnp.concatenate([top, rest], axis=0), high)
            moved = both[0:rows, :] + both[rows:, :] + dot(top, low)
        now = now + moved
    solution[...] = now


def shares_kernel(regime, joints, participation, modes, out):
    depth = modes.shape[0]
    sections, count = out.shape[0] - depth, joints.shape[1]
    out[0:depth, :] = modes[...].astype(f32)
    bucket = lax.broadcasted_iota(jnp.int32, (1, count), 1) // BUCKET
    rate = jnp.zeros((1, count), f32)
    for b in range(count // BUCKET):
        value = jnp.float32(0.0)
        for index, known in enumerate(RATES):
            value = jnp.where(regime[b] == index, jnp.float32(known), value)
        rate = jnp.where(bucket == b, value, rate)
    section = lax.broadcasted_iota(jnp.int32, (sections, count), 0)
    weights = jnp.where(section == joints[...], rate, 0.0)
    squares = participation[...].astype(f32)
    out[depth:, :] = times(split(weights), split(squares * squares))


def modal_kernel(home, a, b, c, d, local, other, whole, payload):
    position, plane = lax.axis_index("sec"), lax.axis_index("mode")
    own = jnp.where(home(position) == plane, a[...], 0.0)
    value = own + b[...] + c[...] + d[...]
    whole[...] = value
    amplitude = jnp.sqrt(jnp.sum(value * value, keepdims=True) / value.size + 1e-06)
    (rows, depth), width = value.shape, local.shape[1]
    sections = local.shape[0] - depth
    rounded = value.astype(bf16)
    for k, source in enumerate((local, other)):
        columns = slice(width * k, width * k + width)
        payload[0:rows, columns] = dot(rounded, source[0:depth, :].astype(bf16))
        payload[rows : rows + sections, columns] = source[depth:, :]
    mine = lax.broadcasted_iota(jnp.int32, (sections, 2 * width), 0) == position
    payload[rows + sections :, :] = jnp.where(mine, amplitude / (1.0 + amplitude), 0.0)


def back_kernel_of(count, *refs):
    plane = lax.axis_index("mode")
    parts, (local, other), (keep, give), scratch = refs[:count], refs[count : count + 2], refs[count + 2 : -1], refs[-1]
    total = parts[0][...]
    for part in parts[1:]:
        total = total + part[...]
    rows, depth = scratch.shape
    sections = (total.shape[0] - rows) // 2
    products = total[rows : rows + sections, :] * total[rows + sections :, :]
    damping = jnp.sum(products, axis=0, keepdims=True)
    removed = (total[0:rows, :] * (damping / (1.0 + damping))).astype(bf16)
    half = local.shape[1]
    scratch[...] = dot_t(removed[:, 0:half], local[0:depth, :].astype(bf16)) + dot_t(
        removed[:, half:], other[0:depth, :].astype(bf16)
    )
    width = keep.shape[1]
    for out, owner in ((keep, plane), (give, plane ^ 2)):
        out[...] = scratch[:, pl.ds(pl.multiple_of(owner * width, width), width)]


def packed_from_hbm(block, thin, packed):
    cells = len(upper(block.shape[0])) + block.shape[0] // TILE
    return pl.pallas_call(
        pack_kernel,
        out_shape=pltpu.VMEM(packed, f32),
        in_specs=[pl.BlockSpec(memory_space=pl.ANY)] * 2,
        out_specs=pl.BlockSpec(memory_space=pltpu.VMEM),
        scratch_shapes=[pltpu.SemaphoreType.DMA((cells,))],
    )(block, thin)


def call(kernel, outs, scratch, args, flops, smem=0, hbm=0):
    vmem, scalar = pl.BlockSpec(memory_space=pltpu.VMEM), pl.BlockSpec(memory_space=pltpu.SMEM)
    moved = sum(a.size * a.dtype.itemsize for a in args) + sum(4 * o[0] * o[1] for o in outs)
    single = len(outs) == 1
    shapes = [jax.ShapeDtypeStruct(o, f32) for o in outs]
    return pl.pallas_call(
        kernel,
        out_shape=shapes[0] if single else tuple(shapes),
        in_specs=[scalar] * smem
        + [vmem] * (len(args) - smem - hbm)
        + [pl.BlockSpec(memory_space=pl.ANY)] * hbm,
        out_specs=vmem if single else tuple([vmem] * len(outs)),
        scratch_shapes=[pltpu.VMEM(s, f32) for s in scratch] + [pltpu.SemaphoreType.DMA] * hbm,
        compiler_params=pltpu.CompilerParams(vmem_limit_bytes=14 << 20),
        cost_estimate=pl.CostEstimate(flops=int(flops), transcendentals=0, bytes_accessed=moved),
    )(*args)


def per_device(coupling, stiffness, loads, modes, joint_section, regime, participation):
    sections, groups = lax.axis_size("sec"), lax.axis_size("mode")
    assert groups == 4 and LEVELS == 3
    size, columns = stiffness.shape[1], loads.shape[1]
    width = size // groups
    cells = len(upper(size))
    packed = (TILE * cells + columns * (size // TILE), TILE)
    square, stacked, thin_shape = (size, size), (size + columns, size), (columns, size)
    product = 0.1 * 6 * size**3
    long = 1.0 * 6 * size**3

    def sent_to(value, where):
        pairs = []
        for s in range(sections):
            for m in range(groups):
                to = where(s, m)
                if to is not None and 0 <= to[0] < sections:
                    pairs.append((s * groups + m, to[0] * groups + to[1]))
        return lax.ppermute(value, AXES, pairs)

    def home(s):
        return 2 * (s % 2) + (s // 2 + s // 4) % 2

    def parity(s, m):
        return m // 2 == s % 2

    block, thin, lower = stiffness[0], loads[0], coupling[0]

    local = call(
        shares_kernel,
        [(size + sections, participation.shape[1])],
        [],
        (regime, joint_section[None, :], participation, modes[0]),
        product // 32,
        smem=1,
    )
    bits = sections.bit_length() - 1
    rounds = [[1]] + [[1 << b, 2 << b, 3 << b] if b + 1 < bits else [1 << b] for b in range(1, bits, 2)]

    def summed_over_sections(value):
        parts = [value]
        for steps in rounds:
            value = parts[0]
            for part in parts[1:]:
                value = value + part
            parts = [value] + [sent_to(value, lambda s, m, k=k: (s ^ k, m)) for k in steps]
        return parts

    packed_down = packed_from_hbm(block, thin, packed)
    lower_sent, packed_down = lax.optimization_barrier((lower, packed_down))
    packed_down = sent_to(packed_down, lambda s, m: (s + 1, m) if parity(s + 1, m) else None)

    def needs_lower(s, m):
        return m == home(s) or (s + 2 < sections and m == home(s + 2))

    lower_down = sent_to(lower_sent, lambda s, m: (s + 1, m) if s >= 1 and needs_lower(s + 1, m) else None)
    lower_up = sent_to(lower_sent, lambda s, m: (s - 1, m) if s >= 1 and m == home(s - 1) else None)
    up = call(
        first_own_kernel, [packed], [stacked, stacked, square], (block, thin, lower), 6 * product, hbm=1
    )
    up = sent_to(up, lambda s, m: (s - 1, m) if parity(s - 1, m) else None)
    other = sent_to(local, lambda s, m: (s, m ^ 1))
    through, full = call(
        first_receive_kernel, [square, stacked], [stacked, square, square], (packed_down, lower), 6 * long, hbm=1
    )
    sent, block, thin = call(fold_kernel, [packed, square, thin_shape], [], (block, thin, full, up), 0)

    packed_down = sent_to(sent, lambda s, m: (s + 2, m) if m == home(s + 2) else None)
    up, done = call(
        bracket_kernel, [packed, (8, TILE)], [stacked, stacked], (block, thin, through), 6 * product
    )
    up = sent_to(up, lambda s, m: (s - 2, m) if m == home(s - 2) else None)
    lower_down, other = lax.optimization_barrier((lower_down, other))
    lower = call(lower_kernel, [square], [], (through, lower_down, done), product)
    lower_down = sent_to(lower, lambda s, m: (s + 2, m) if s >= 2 and m == home(s + 2) else None)
    packed_down, lower_up = lax.optimization_barrier((packed_down, lower_up))
    through, full = call(receive_kernel, [square, stacked], [stacked, square], (packed_down, lower), 60 * product)
    sent, block, thin = call(
        fold_above_kernel,
        [packed, square, thin_shape],
        [stacked, stacked, square],
        (up, lower_up, block, thin, full),
        2 * long,
    )

    sent, lower_down = lax.optimization_barrier((sent, lower_down))
    packed_down = sent_to(sent, lambda s, m: (s + 4, home(s + 4)) if m == home(s) else None)
    has_before = lambda: lax.axis_index("sec") >= 4
    inverse = call(functools.partial(whole_inverse_kernel, has_before), [square], [], (block,), 4 * long)
    lower, up = call(
        functools.partial(last_lower_kernel, has_before), [square, packed], [stacked, stacked], (through, lower_down, inverse, thin), 3 * product
    )
    up = sent_to(up, lambda s, m: (s - 4, home(s - 4)) if m == home(s) else None)
    block, thin = call(
        functools.partial(last_receive_kernel, has_before),
        [square, thin_shape],
        [stacked, square],
        (packed_down, lower, block, thin),
        6 * product,
    )
    solved = call(solve_kernel, [thin_shape], [square, thin_shape], (block, thin, up), product)

    parts = [
        sent_to(solved, lambda s, m, k=k: (s, (m + k) % groups) if m == home(s) else None)
        for k in range(1, groups)
    ]
    whole, payload = call(
        functools.partial(modal_kernel, home),
        [thin_shape, (columns + 2 * sections, 2 * modes.shape[2])],
        [],
        (solved, *parts, local, other),
        product // 32,
    )
    parts = summed_over_sections(payload)
    keep, give = call(
        functools.partial(back_kernel_of, len(parts)),
        [(columns, width)] * 2,
        [thin_shape],
        (*parts, local, other),
        product // 32,
    )
    summed = keep + sent_to(give, lambda s, m: (s, m ^ 2))
    own_columns = lax.dynamic_slice_in_dim(whole, lax.axis_index("mode") * width, width, 1)
    return (own_columns[None], (own_columns - summed)[None])


def solution(mesh):
    in_specs = (
        P("sec", None, None),
        P("sec", None, None),
        P("sec", None, None),
        P("sec", None, "mode"),
        P("sec"),
        P("sec"),
        P("sec", "mode"),
    )
    out_specs = (P("sec", None, "mode"), P("sec", None, "mode"))
    return jax.shard_map(
        per_device, mesh=mesh, in_specs=in_specs, out_specs=out_specs, check_vma=False
    )
```

```python
import functools

import jax
import jax.numpy as jnp
from jax import lax
from jax.experimental import pallas as pl
from jax.experimental.pallas import tpu as pltpu
from jax.sharding import PartitionSpec as P

LEVELS = 3
BUCKET = 64
RATES = (0.2, 0.5, 1.0, 2.0)
AXES = ("sec", "mode")
TILE = 128
f32, bf16 = jnp.float32, jnp.bfloat16


def split(value):
    high = value.astype(bf16)
    return high, (value - high.astype(f32)).astype(bf16)


def dot(left, right):
    return jnp.dot(left, right, preferred_element_type=f32)


def dot_t(left, right):
    return lax.dot_general(left, right, (((1,), (1,)), ((), ())), preferred_element_type=f32)


def times(left, right, product=dot):
    return product(left[0], right[0]) + product(left[0], right[1]) + product(left[1], right[0])


def upper(size):
    count = size // TILE
    return [(a, b) for a in range(count) for b in range(a, count)]


def band(index):
    return slice(TILE * index, TILE * index + TILE)


def unpack(packed, block, thin):
    size = block.shape[0]
    cells = upper(size)
    for index, (a, b) in enumerate(cells):
        cell = packed[band(index), :]
        block[band(a), band(b)] = cell
        if a != b:
            block[band(b), band(a)] = cell.T
    rows = thin.shape[0]
    for c in range(size // TILE):
        start = TILE * len(cells) + rows * c
        thin[:, band(c)] = packed[start : start + rows, :]


def pack(packed, block, thin):
    size = block.shape[1]
    cells = upper(size)
    for index, (a, b) in enumerate(cells):
        packed[band(index), :] = block[band(a), band(b)]
    rows = thin.shape[0]
    for c in range(size // TILE):
        start = TILE * len(cells) + rows * c
        packed[start : start + rows, :] = thin[:, band(c)]


def scaled(block):
    size = block.shape[0]
    eye = lax.broadcasted_iota(jnp.int32, (size, size), 0) == lax.broadcasted_iota(
        jnp.int32, (size, size), 1
    )
    only = jnp.where(eye, block, 0.0)
    down = jnp.sum(only, axis=1, keepdims=True)
    along = jnp.sum(only, axis=0, keepdims=True)
    down = jnp.where(down == 0.0, 0.0, 1.0 / down)
    along = jnp.where(along == 0.0, 0.0, 1.0 / along)
    unit = jnp.where(eye, 1.0, 0.0)
    return unit, down, along, unit - down * block


def inverse_of(block):
    unit, down, along, first = scaled(block)
    one = split(first)
    second = times(one, one)
    two = split(second)
    third = dot(one[0], two[0])
    fourth = dot(two[0], two[0]).astype(bf16)
    series = unit + first + second + third
    series = series + dot(series.astype(bf16), fourth)
    return series * along


def schur(rows_and_thin, inverse, right, product):
    through = times(split(rows_and_thin), split(inverse))
    return through, times(split(through), split(right), product)


def pack_kernel(block, thin, packed, sems):
    size = block.shape[0]
    cells = upper(size)
    rows = thin.shape[0]
    pairs = [
        (block.at[band(a), band(b)], packed.at[band(index), :]) for index, (a, b) in enumerate(cells)
    ]
    for c in range(size // TILE):
        start = TILE * len(cells) + rows * c
        pairs.append((thin.at[:, band(c)], packed.at[start : start + rows, :]))
    copies = [pltpu.make_async_copy(src, dst, sems.at[k]) for k, (src, dst) in enumerate(pairs)]
    for copy in copies:
        copy.start()
    for copy in copies:
        copy.wait()


def folded(packed, block, thin, *others):
    size = block.shape[0]
    cells = upper(size)
    for index, (a, b) in enumerate(cells):
        value = block[band(a), band(b)]
        for other in others:
            same = other.shape == packed.shape
            value = value - (other[band(index), :] if same else other[band(a), band(b)])
        packed[band(index), :] = value
    rows = thin.shape[0]
    for c in range(size // TILE):
        start = TILE * len(cells) + rows * c
        value = thin[:, band(c)]
        for other in others:
            same = other.shape == packed.shape
            value = value - (other[start : start + rows, :] if same else other[size:, band(c)])
        packed[start : start + rows, :] = value


def first_own_kernel(block, thin, lower_hbm, packed, stack, out, lower, sem):
    copy = pltpu.make_async_copy(lower_hbm, lower, sem)
    copy.start()
    own_kernel(block, thin, lower, packed, stack, out, copy)


def own_kernel(block, thin, lower, packed, stack, out, copy=None):
    size = block.shape[0]
    inverse = inverse_of(block[...])
    if copy is not None:
        copy.wait()
    stack[0:size, :] = lower[...].T
    stack[size:, :] = thin[...]
    _, out[...] = schur(stack[...], inverse, lower[...], dot)
    pack(packed, out, out.at[size:, :])


def bracket_kernel(block, thin, lower, packed, done, stack, out):
    own_kernel(block, thin, lower, packed, stack, out)
    done[...] = jnp.zeros_like(done)


def first_receive_kernel(packed, lower_hbm, through, full, stack, whole, lower, sem):
    copy = pltpu.make_async_copy(lower_hbm, lower, sem)
    copy.start()
    receive_kernel(packed, lower, through, full, stack, whole, copy)


def receive_kernel(packed, lower, through, full, stack, whole, copy=None):
    size = lower.shape[0]
    unpack(packed, whole, stack.at[size:, :])
    inverse = inverse_of(whole[...])
    if copy is not None:
        copy.wait()
    stack[0:size, :] = lower[...]
    half, full[...] = schur(stack[...], inverse, lower[...], dot_t)
    through[...] = half[0:size, :]


def fold_kernel(block, thin, full, above, packed, block_out, thin_out):
    folded(packed, block, thin, full, above)
    unpack(packed, block_out, thin_out)


def part_above(packed_above, passed, stack, out, whole):
    size = passed.shape[0]
    unpack(packed_above, whole, stack.at[size:, :])
    right = split(passed[...])
    stack[0:size, :] = times(split(passed[...].T), split(whole[...]))
    stack[size:, :] = -stack[size:, :]
    out[...] = times(split(stack[...]), right)


def fold_above_kernel(early, late, passed, block, thin, full, packed, block_out, thin_out, stack, out, whole, both):
    both[...] = early[...] + late[...]
    part_above(both, passed, stack, out, whole)
    folded(packed, block, thin, full, out)
    unpack(packed, block_out, thin_out)


def fold_sent_kernel(needed, after, early, late, passed, block, thin, full, packed, block_out, thin_out, *scratch):
    @pl.when(needed())
    def _():
        fold_above_kernel(early, late, passed, block, thin, full, packed, block_out, thin_out, *scratch)


def fold_kept_kernel(needed, early, passed, block, thin, full, block_out, thin_out, inverse, stack, out, whole):
    size = block.shape[0]

    @pl.when(needed())
    def _():
        part_above(early, passed, stack, out, whole)
        value = block[...] - full[0:size, :] - out[0:size, :]
        block_out[...] = value
        thin_out[...] = thin[...] - full[size:, :] - out[size:, :]
        inverse[...] = inverse_of(value)


def whole_inverse_kernel(needed, block, inverse):
    @pl.when(needed())
    def _():
        inverse[...] = inverse_of(block[...])


def lower_kernel(through, passed, after, lower):
    lower[...] = -times(split(through[...]), split(passed[...]))


def last_lower_kernel(needed, through, passed, inverse, thin, lower, packed, stack, out):
    size = inverse.shape[0]

    @pl.when(needed())
    def _():
        value = -times(split(through[...]), split(passed[...]))
        lower[...] = value
        stack[0:size, :] = value.T
        stack[size:, :] = thin[...]
        _, out[...] = schur(stack[...], inverse[...], value, dot)
        pack(packed, out, out.at[size:, :])


def last_receive_kernel(needed, packed, lower, block, thin, block_else, thin_else, block_out, thin_out, stack, whole):
    size = block.shape[0]

    @pl.when(needed())
    def _():
        unpack(packed, whole, stack.at[size:, :])
        inverse = inverse_of(whole[...])
        stack[0:size, :] = lower[...]
        _, full = schur(stack[...], inverse, lower[...], dot_t)
        block_out[...] = block[...] - full[0:size, :]
        thin_out[...] = thin[...] - full[size:, :]

    @pl.when(jnp.logical_not(needed()))
    def _():
        block_out[...] = block_else[...]
        thin_out[...] = thin_else[...]


def solve_kernel(block, thin, above, solution, whole, own):
    unpack(above, whole, own)
    value = block[...] - whole[...]
    unit, _, along, _ = scaled(value)
    high, low = split(unit - value * along)
    rows = thin.shape[0]
    now = (thin[...] - own[...]) * along
    for power in (1, 2, 4):
        moved = now
        for _ in range(power):
            top, rest = split(moved)
            both = dot(jnp.concatenate([top, rest], axis=0), high)
            moved = both[0:rows, :] + both[rows:, :] + dot(top, low)
        now = now + moved
    solution[...] = now


def shares_kernel(regime, joints, participation, modes, out):
    depth = modes.shape[0]
    sections, count = out.shape[0] - depth, joints.shape[1]
    out[0:depth, :] = modes[...].astype(f32)
    bucket = lax.broadcasted_iota(jnp.int32, (1, count), 1) // BUCKET
    rate = jnp.zeros((1, count), f32)
    for b in range(count // BUCKET):
        value = jnp.float32(0.0)
        for index, known in enumerate(RATES):
            value = jnp.where(regime[b] == index, jnp.float32(known), value)
        rate = jnp.where(bucket == b, value, rate)
    section = lax.broadcasted_iota(jnp.int32, (sections, count), 0)
    weights = jnp.where(section == joints[...], rate, 0.0)
    squares = participation[...].astype(f32)
    out[depth:, :] = times(split(weights), split(squares * squares))


def modal_kernel(home, a, b, c, d, local, other, whole, payload):
    position, plane = lax.axis_index("sec"), lax.axis_index("mode")
    own = jnp.where(home(position) == plane, a[...], 0.0)
    value = own + b[...] + c[...] + d[...]
    whole[...] = value
    amplitude = jnp.sqrt(jnp.sum(value * value, keepdims=True) / value.size + 1e-06)
    (rows, depth), width = value.shape, local.shape[1]
    sections = local.shape[0] - depth
    rounded = value.astype(bf16)
    for k, source in enumerate((local, other)):
        columns = slice(width * k, width * k + width)
        payload[0:rows, columns] = dot(rounded, source[0:depth, :].astype(bf16))
        payload[rows : rows + sections, columns] = source[depth:, :]
    mine = lax.broadcasted_iota(jnp.int32, (sections, 2 * width), 0) == position
    payload[rows + sections :, :] = jnp.where(mine, amplitude / (1.0 + amplitude), 0.0)


def back_kernel_of(count, *refs):
    plane = lax.axis_index("mode")
    parts, (local, other), (keep, give), scratch = refs[:count], refs[count : count + 2], refs[count + 2 : -1], refs[-1]
    total = parts[0][...]
    for part in parts[1:]:
        total = total + part[...]
    rows, depth = scratch.shape
    sections = (total.shape[0] - rows) // 2
    products = total[rows : rows + sections, :] * total[rows + sections :, :]
    damping = jnp.sum(products, axis=0, keepdims=True)
    removed = (total[0:rows, :] * (damping / (1.0 + damping))).astype(bf16)
    half = local.shape[1]
    scratch[...] = dot_t(removed[:, 0:half], local[0:depth, :].astype(bf16)) + dot_t(
        removed[:, half:], other[0:depth, :].astype(bf16)
    )
    width = keep.shape[1]
    for out, owner in ((keep, plane), (give, plane ^ 2)):
        out[...] = scratch[:, pl.ds(pl.multiple_of(owner * width, width), width)]


def packed_from_hbm(block, thin, packed):
    cells = len(upper(block.shape[0])) + block.shape[0] // TILE
    return pl.pallas_call(
        pack_kernel,
        out_shape=pltpu.VMEM(packed, f32),
        in_specs=[pl.BlockSpec(memory_space=pl.ANY)] * 2,
        out_specs=pl.BlockSpec(memory_space=pltpu.VMEM),
        scratch_shapes=[pltpu.SemaphoreType.DMA((cells,))],
    )(block, thin)


def call(kernel, outs, scratch, args, flops, smem=0, hbm=0):
    vmem, scalar = pl.BlockSpec(memory_space=pltpu.VMEM), pl.BlockSpec(memory_space=pltpu.SMEM)
    moved = sum(a.size * a.dtype.itemsize for a in args) + sum(4 * o[0] * o[1] for o in outs)
    single = len(outs) == 1
    shapes = [jax.ShapeDtypeStruct(o, f32) for o in outs]
    return pl.pallas_call(
        kernel,
        out_shape=shapes[0] if single else tuple(shapes),
        in_specs=[scalar] * smem
        + [vmem] * (len(args) - smem - hbm)
        + [pl.BlockSpec(memory_space=pl.ANY)] * hbm,
        out_specs=vmem if single else tuple([vmem] * len(outs)),
        scratch_shapes=[pltpu.VMEM(s, f32) for s in scratch] + [pltpu.SemaphoreType.DMA] * hbm,
        compiler_params=pltpu.CompilerParams(vmem_limit_bytes=14 << 20),
        cost_estimate=pl.CostEstimate(flops=int(flops), transcendentals=0, bytes_accessed=moved),
    )(*args)


def per_device(coupling, stiffness, loads, modes, joint_section, regime, participation):
    sections, groups = lax.axis_size("sec"), lax.axis_size("mode")
    assert groups == 4 and LEVELS == 3
    size, columns = stiffness.shape[1], loads.shape[1]
    width = size // groups
    cells = len(upper(size))
    packed = (TILE * cells + columns * (size // TILE), TILE)
    square, stacked, thin_shape = (size, size), (size + columns, size), (columns, size)
    product = 0.1 * 6 * size**3
    long = 1.0 * 6 * size**3

    def sent_to(value, where):
        pairs = []
        for s in range(sections):
            for m in range(groups):
                to = where(s, m)
                if to is not None and 0 <= to[0] < sections:
                    pairs.append((s * groups + m, to[0] * groups + to[1]))
        return lax.ppermute(value, AXES, pairs)

    def home(s):
        return 2 * (s % 2) + (s // 2 + s // 4) % 2

    def parity(s, m):
        return m // 2 == s % 2

    block, thin, lower = stiffness[0], loads[0], coupling[0]

    local = call(
        shares_kernel,
        [(size + sections, participation.shape[1])],
        [],
        (regime, joint_section[None, :], participation, modes[0]),
        product // 32,
        smem=1,
    )
    bits = sections.bit_length() - 1
    rounds = [[1]] + [[1 << b, 2 << b, 3 << b] if b + 1 < bits else [1 << b] for b in range(1, bits, 2)]

    def summed_over_sections(value):
        parts = [value]
        for steps in rounds:
            value = parts[0]
            for part in parts[1:]:
                value = value + part
            parts = [value] + [sent_to(value, lambda s, m, k=k: (s ^ k, m)) for k in steps]
        return parts

    packed_down = packed_from_hbm(block, thin, packed)
    lower_sent, packed_down = lax.optimization_barrier((lower, packed_down))
    packed_down = sent_to(packed_down, lambda s, m: (s + 1, m) if parity(s + 1, m) else None)

    def needs_lower(s, m):
        return m == home(s) or (s + 2 < sections and m == home(s + 2))

    lower_down = sent_to(lower_sent, lambda s, m: (s + 1, m) if s >= 1 and needs_lower(s + 1, m) else None)
    lower_up = sent_to(lower_sent, lambda s, m: (s - 1, m) if s >= 1 and m == home(s - 1) else None)
    up = call(
        first_own_kernel, [packed], [stacked, stacked, square], (block, thin, lower), 6 * product, hbm=1
    )
    up = sent_to(up, lambda s, m: (s - 1, m) if parity(s - 1, m) else None)
    other = sent_to(local, lambda s, m: (s, m ^ 1))
    through, full = call(
        first_receive_kernel, [square, stacked], [stacked, square, square], (packed_down, lower), 6 * long, hbm=1
    )
    sent, block, thin = call(fold_kernel, [packed, square, thin_shape], [], (block, thin, full, up), 0)

    packed_down = sent_to(sent, lambda s, m: (s + 2, m) if m == home(s + 2) else None)
    up, done = call(
        bracket_kernel, [packed, (8, TILE)], [stacked, stacked], (block, thin, through), 6 * product
    )
    early = sent_to(up, lambda s, m: (s - 2, m) if m == home(s - 2) and m != home(s) else None)
    up_late = up
    lower_down, other = lax.optimization_barrier((lower_down, other))
    lower = call(lower_kernel, [square], [], (through, lower_down, done), product)
    lower_down = sent_to(lower, lambda s, m: (s + 2, m) if s >= 2 and m == home(s + 2) else None)
    up_late, _ = lax.optimization_barrier((up_late, lower))
    late = sent_to(up_late, lambda s, m: (s - 2, m) if m == home(s - 2) and m == home(s) else None)
    packed_down, lower_up = lax.optimization_barrier((packed_down, lower_up))
    through, full = call(receive_kernel, [square, stacked], [stacked, square], (packed_down, lower), 6 * product)
    has_before = lambda: lax.axis_index("sec") >= 4
    if sections == 8:
        block_kept, thin_kept, inverse = call(
            functools.partial(fold_kept_kernel, has_before),
            [square, thin_shape, square],
            [stacked, stacked, square],
            (early, lower_up, block, thin, full),
            2 * long,
        )
        sent, block, thin = call(
            functools.partial(fold_sent_kernel, lambda: lax.axis_index("sec") < 4),
            [packed, square, thin_shape],
            [stacked, stacked, square, packed],
            (thin_kept, early, late, lower_up, block, thin, full),
            3 * long,
        )
    else:
        sent, block, thin = call(
            fold_above_kernel,
            [packed, square, thin_shape],
            [stacked, stacked, square, packed],
            (early, late, lower_up, block, thin, full),
            2 * long,
        )
        inverse = call(functools.partial(whole_inverse_kernel, has_before), [square], [], (block,), 4 * long)
        block_kept, thin_kept = block, thin

    sent, lower_down = lax.optimization_barrier((sent, lower_down))
    packed_down = sent_to(sent, lambda s, m: (s + 4, home(s + 4)) if m == home(s) else None)
    lower, up = call(
        functools.partial(last_lower_kernel, has_before), [square, packed], [stacked, stacked], (through, lower_down, inverse, thin_kept), 3 * product
    )
    up = sent_to(up, lambda s, m: (s - 4, home(s - 4)) if m == home(s) else None)
    block, thin = call(
        functools.partial(last_receive_kernel, has_before),
        [square, thin_shape],
        [stacked, square],
        (packed_down, lower, block_kept, thin_kept, block, thin),
        6 * product,
    )
    solved = call(solve_kernel, [thin_shape], [square, thin_shape], (block, thin, up), product)

    parts = [
        sent_to(solved, lambda s, m, k=k: (s, (m + k) % groups) if m == home(s) else None)
        for k in range(1, groups)
    ]
    whole, payload = call(
        functools.partial(modal_kernel, home),
        [thin_shape, (columns + 2 * sections, 2 * modes.shape[2])],
        [],
        (solved, *parts, local, other),
        product // 32,
    )
    parts = summed_over_sections(payload)
    keep, give = call(
        functools.partial(back_kernel_of, len(parts)),
        [(columns, width)] * 2,
        [thin_shape],
        (*parts, local, other),
        product // 32,
    )
    summed = keep + sent_to(give, lambda s, m: (s, m ^ 2))
    own_columns = lax.dynamic_slice_in_dim(whole, lax.axis_index("mode") * width, width, 1)
    return (own_columns[None], (own_columns - summed)[None])


def solution(mesh):
    in_specs = (
        P("sec", None, None),
        P("sec", None, None),
        P("sec", None, None),
        P("sec", None, "mode"),
        P("sec"),
        P("sec"),
        P("sec", "mode"),
    )
    out_specs = (P("sec", None, "mode"), P("sec", None, "mode"))
    return jax.shard_map(
        per_device, mesh=mesh, in_specs=in_specs, out_specs=out_specs, check_vma=False
    )
```

```python
import functools

import jax
import jax.numpy as jnp
from jax import lax
from jax.experimental import pallas as pl
from jax.experimental.pallas import tpu as pltpu
from jax.sharding import PartitionSpec as P

LEVELS = 3
BUCKET = 64
RATES = (0.2, 0.5, 1.0, 2.0)
AXES = ("sec", "mode")
TILE = 128
f32, bf16 = jnp.float32, jnp.bfloat16


def split(value):
    high = value.astype(bf16)
    return high, (value - high.astype(f32)).astype(bf16)


def dot(left, right):
    return jnp.dot(left, right, preferred_element_type=f32)


def dot_t(left, right):
    return lax.dot_general(left, right, (((1,), (1,)), ((), ())), preferred_element_type=f32)


def times(left, right, product=dot):
    return product(left[0], right[0]) + product(left[0], right[1]) + product(left[1], right[0])


def upper(size):
    count = size // TILE
    return [(a, b) for a in range(count) for b in range(a, count)]


def band(index):
    return slice(TILE * index, TILE * index + TILE)


def unpack(packed, block, thin):
    size = block.shape[0]
    cells = upper(size)
    for index, (a, b) in enumerate(cells):
        cell = packed[band(index), :]
        block[band(a), band(b)] = cell
        if a != b:
            block[band(b), band(a)] = cell.T
    rows = thin.shape[0]
    for c in range(size // TILE):
        start = TILE * len(cells) + rows * c
        thin[:, band(c)] = packed[start : start + rows, :]


def pack(packed, block, thin):
    size = block.shape[1]
    cells = upper(size)
    for index, (a, b) in enumerate(cells):
        packed[band(index), :] = block[band(a), band(b)]
    rows = thin.shape[0]
    for c in range(size // TILE):
        start = TILE * len(cells) + rows * c
        packed[start : start + rows, :] = thin[:, band(c)]


def scaled(block):
    size = block.shape[0]
    eye = lax.broadcasted_iota(jnp.int32, (size, size), 0) == lax.broadcasted_iota(
        jnp.int32, (size, size), 1
    )
    only = jnp.where(eye, block, 0.0)
    down = jnp.sum(only, axis=1, keepdims=True)
    along = jnp.sum(only, axis=0, keepdims=True)
    down = jnp.where(down == 0.0, 0.0, 1.0 / down)
    along = jnp.where(along == 0.0, 0.0, 1.0 / along)
    unit = jnp.where(eye, 1.0, 0.0)
    return unit, down, along, unit - down * block


def inverse_of(block):
    unit, down, along, first = scaled(block)
    one = split(first)
    second = times(one, one)
    two = split(second)
    third = dot(one[0], two[0])
    fourth = dot(two[0], two[0]).astype(bf16)
    series = unit + first + second + third
    series = series + dot(series.astype(bf16), fourth)
    return series * along


def schur(rows_and_thin, inverse, right, product):
    through = times(split(rows_and_thin), split(inverse))
    return through, times(split(through), split(right), product)


def pack_kernel(block, thin, packed, sems):
    size = block.shape[0]
    cells = upper(size)
    rows = thin.shape[0]
    pairs = [
        (block.at[band(a), band(b)], packed.at[band(index), :]) for index, (a, b) in enumerate(cells)
    ]
    for c in range(size // TILE):
        start = TILE * len(cells) + rows * c
        pairs.append((thin.at[:, band(c)], packed.at[start : start + rows, :]))
    copies = [pltpu.make_async_copy(src, dst, sems.at[k]) for k, (src, dst) in enumerate(pairs)]
    for copy in copies:
        copy.start()
    for copy in copies:
        copy.wait()


def folded(packed, block, thin, *others):
    size = block.shape[0]
    cells = upper(size)
    for index, (a, b) in enumerate(cells):
        value = block[band(a), band(b)]
        for other in others:
            same = other.shape == packed.shape
            value = value - (other[band(index), :] if same else other[band(a), band(b)])
        packed[band(index), :] = value
    rows = thin.shape[0]
    for c in range(size // TILE):
        start = TILE * len(cells) + rows * c
        value = thin[:, band(c)]
        for other in others:
            same = other.shape == packed.shape
            value = value - (other[start : start + rows, :] if same else other[size:, band(c)])
        packed[start : start + rows, :] = value


def first_own_kernel(both, lower_hbm, packed, stack, out, lower, whole, thin, sem):
    copy = pltpu.make_async_copy(lower_hbm, lower, sem)
    copy.start()
    unpack(both, whole, thin)
    own_kernel(whole, thin, lower, packed, stack, out, copy)


def own_kernel(block, thin, lower, packed, stack, out, copy=None):
    size = block.shape[0]
    inverse = inverse_of(block[...])
    if copy is not None:
        copy.wait()
    stack[0:size, :] = lower[...].T
    stack[size:, :] = thin[...]
    _, out[...] = schur(stack[...], inverse, lower[...], dot)
    pack(packed, out, out.at[size:, :])


def bracket_kernel(block, thin, lower, packed, done, stack, out):
    own_kernel(block, thin, lower, packed, stack, out)
    done[...] = jnp.zeros_like(done)


def first_receive_kernel(packed, lower_hbm, through, full, stack, whole, lower, sem):
    copy = pltpu.make_async_copy(lower_hbm, lower, sem)
    copy.start()
    receive_kernel(packed, lower, through, full, stack, whole, copy)


def receive_kernel(packed, lower, through, full, stack, whole, copy=None):
    size = lower.shape[0]
    unpack(packed, whole, stack.at[size:, :])
    inverse = inverse_of(whole[...])
    if copy is not None:
        copy.wait()
    stack[0:size, :] = lower[...]
    half, full[...] = schur(stack[...], inverse, lower[...], dot_t)
    through[...] = half[0:size, :]


def fold_kernel(both, full, above, packed, block_out, thin_out):
    unpack(both, block_out, thin_out)
    folded(packed, block_out, thin_out, full, above)
    unpack(packed, block_out, thin_out)


def part_above(packed_above, passed, stack, out, whole):
    size = passed.shape[0]
    unpack(packed_above, whole, stack.at[size:, :])
    right = split(passed[...])
    stack[0:size, :] = times(split(passed[...].T), split(whole[...]))
    stack[size:, :] = -stack[size:, :]
    out[...] = times(split(stack[...]), right)


def fold_above_kernel(early, late, passed, block, thin, full, packed, block_out, thin_out, stack, out, whole, both):
    both[...] = early[...] + late[...]
    part_above(both, passed, stack, out, whole)
    folded(packed, block, thin, full, out)
    unpack(packed, block_out, thin_out)


def fold_sent_kernel(needed, after, early, late, passed, block, thin, full, packed, block_out, thin_out, *scratch):
    @pl.when(needed())
    def _():
        fold_above_kernel(early, late, passed, block, thin, full, packed, block_out, thin_out, *scratch)


def fold_kept_kernel(needed, early, passed, block, thin, full, block_out, thin_out, inverse, stack, out, whole):
    size = block.shape[0]

    @pl.when(needed())
    def _():
        part_above(early, passed, stack, out, whole)
        value = block[...] - full[0:size, :] - out[0:size, :]
        block_out[...] = value
        thin_out[...] = thin[...] - full[size:, :] - out[size:, :]
        inverse[...] = inverse_of(value)


def whole_inverse_kernel(needed, block, inverse):
    @pl.when(needed())
    def _():
        inverse[...] = inverse_of(block[...])


def lower_kernel(through, passed, after, lower):
    lower[...] = -times(split(through[...]), split(passed[...]))


def last_lower_kernel(needed, through, passed, inverse, thin, lower, packed, stack, out):
    size = inverse.shape[0]

    @pl.when(needed())
    def _():
        value = -times(split(through[...]), split(passed[...]))
        lower[...] = value
        stack[0:size, :] = value.T
        stack[size:, :] = thin[...]
        _, out[...] = schur(stack[...], inverse[...], value, dot)
        pack(packed, out, out.at[size:, :])


def last_receive_kernel(needed, packed, lower, block, thin, block_else, thin_else, block_out, thin_out, stack, whole):
    size = block.shape[0]

    @pl.when(needed())
    def _():
        unpack(packed, whole, stack.at[size:, :])
        inverse = inverse_of(whole[...])
        stack[0:size, :] = lower[...]
        _, full = schur(stack[...], inverse, lower[...], dot_t)
        block_out[...] = block[...] - full[0:size, :]
        thin_out[...] = thin[...] - full[size:, :]

    @pl.when(jnp.logical_not(needed()))
    def _():
        block_out[...] = block_else[...]
        thin_out[...] = thin_else[...]


def solve_kernel(block, thin, above, solution, whole, own):
    unpack(above, whole, own)
    value = block[...] - whole[...]
    unit, _, along, _ = scaled(value)
    high, low = split(unit - value * along)
    rows = thin.shape[0]
    now = (thin[...] - own[...]) * along
    for power in (1, 2, 4):
        moved = now
        for _ in range(power):
            top, rest = split(moved)
            both = dot(jnp.concatenate([top, rest], axis=0), high)
            moved = both[0:rows, :] + both[rows:, :] + dot(top, low)
        now = now + moved
    solution[...] = now


def shares_kernel(regime, joints, participation, modes, out):
    depth = modes.shape[0]
    sections, count = out.shape[0] - depth, joints.shape[1]
    out[0:depth, :] = modes[...].astype(f32)
    bucket = lax.broadcasted_iota(jnp.int32, (1, count), 1) // BUCKET
    rate = jnp.zeros((1, count), f32)
    for b in range(count // BUCKET):
        value = jnp.float32(0.0)
        for index, known in enumerate(RATES):
            value = jnp.where(regime[b] == index, jnp.float32(known), value)
        rate = jnp.where(bucket == b, value, rate)
    section = lax.broadcasted_iota(jnp.int32, (sections, count), 0)
    weights = jnp.where(section == joints[...], rate, 0.0)
    squares = participation[...].astype(f32)
    out[depth:, :] = times(split(weights), split(squares * squares))


def modal_kernel(home, a, b, c, d, local, other, whole, payload):
    position, plane = lax.axis_index("sec"), lax.axis_index("mode")
    own = jnp.where(home(position) == plane, a[...], 0.0)
    value = own + b[...] + c[...] + d[...]
    whole[...] = value
    amplitude = jnp.sqrt(jnp.sum(value * value, keepdims=True) / value.size + 1e-06)
    (rows, depth), width = value.shape, local.shape[1]
    sections = local.shape[0] - depth
    rounded = value.astype(bf16)
    for k, source in enumerate((local, other)):
        columns = slice(width * k, width * k + width)
        payload[0:rows, columns] = dot(rounded, source[0:depth, :].astype(bf16))
        payload[rows : rows + sections, columns] = source[depth:, :]
    mine = lax.broadcasted_iota(jnp.int32, (sections, 2 * width), 0) == position
    payload[rows + sections :, :] = jnp.where(mine, amplitude / (1.0 + amplitude), 0.0)


def back_kernel_of(count, *refs):
    plane = lax.axis_index("mode")
    parts, (local, other), (keep, give), scratch = refs[:count], refs[count : count + 2], refs[count + 2 : -1], refs[-1]
    total = parts[0][...]
    for part in parts[1:]:
        total = total + part[...]
    rows, depth = scratch.shape
    sections = (total.shape[0] - rows) // 2
    products = total[rows : rows + sections, :] * total[rows + sections :, :]
    damping = jnp.sum(products, axis=0, keepdims=True)
    removed = (total[0:rows, :] * (damping / (1.0 + damping))).astype(bf16)
    half = local.shape[1]
    scratch[...] = dot_t(removed[:, 0:half], local[0:depth, :].astype(bf16)) + dot_t(
        removed[:, half:], other[0:depth, :].astype(bf16)
    )
    width = keep.shape[1]
    for out, owner in ((keep, plane), (give, plane ^ 2)):
        out[...] = scratch[:, pl.ds(pl.multiple_of(owner * width, width), width)]


def packed_from_hbm(block, thin, packed):
    cells = len(upper(block.shape[0])) + block.shape[0] // TILE
    return pl.pallas_call(
        pack_kernel,
        out_shape=pltpu.VMEM(packed, f32),
        in_specs=[pl.BlockSpec(memory_space=pl.ANY)] * 2,
        out_specs=pl.BlockSpec(memory_space=pltpu.VMEM),
        scratch_shapes=[pltpu.SemaphoreType.DMA((cells,))],
    )(block, thin)


def call(kernel, outs, scratch, args, flops, smem=0, hbm=0):
    vmem, scalar = pl.BlockSpec(memory_space=pltpu.VMEM), pl.BlockSpec(memory_space=pltpu.SMEM)
    moved = sum(a.size * a.dtype.itemsize for a in args) + sum(4 * o[0] * o[1] for o in outs)
    single = len(outs) == 1
    shapes = [jax.ShapeDtypeStruct(o, f32) for o in outs]
    return pl.pallas_call(
        kernel,
        out_shape=shapes[0] if single else tuple(shapes),
        in_specs=[scalar] * smem
        + [vmem] * (len(args) - smem - hbm)
        + [pl.BlockSpec(memory_space=pl.ANY)] * hbm,
        out_specs=vmem if single else tuple([vmem] * len(outs)),
        scratch_shapes=[pltpu.VMEM(s, f32) for s in scratch] + [pltpu.SemaphoreType.DMA] * hbm,
        compiler_params=pltpu.CompilerParams(vmem_limit_bytes=14 << 20),
        cost_estimate=pl.CostEstimate(flops=int(flops), transcendentals=0, bytes_accessed=moved),
    )(*args)


def per_device(coupling, stiffness, loads, modes, joint_section, regime, participation):
    sections, groups = lax.axis_size("sec"), lax.axis_size("mode")
    assert groups == 4 and LEVELS == 3
    size, columns = stiffness.shape[1], loads.shape[1]
    width = size // groups
    cells = len(upper(size))
    packed = (TILE * cells + columns * (size // TILE), TILE)
    square, stacked, thin_shape = (size, size), (size + columns, size), (columns, size)
    product = 0.1 * 6 * size**3
    long = 1.0 * 6 * size**3

    def sent_to(value, where):
        pairs = []
        for s in range(sections):
            for m in range(groups):
                to = where(s, m)
                if to is not None and 0 <= to[0] < sections:
                    pairs.append((s * groups + m, to[0] * groups + to[1]))
        return lax.ppermute(value, AXES, pairs)

    def home(s):
        return 2 * (s % 2) + (s // 2 + s // 4) % 2

    def parity(s, m):
        return m // 2 == s % 2

    block, thin, lower = stiffness[0], loads[0], coupling[0]

    local = call(
        shares_kernel,
        [(size + sections, participation.shape[1])],
        [],
        (regime, joint_section[None, :], participation, modes[0]),
        product // 32,
        smem=1,
    )
    bits = sections.bit_length() - 1
    rounds = [[1]] + [[1 << b, 2 << b, 3 << b] if b + 1 < bits else [1 << b] for b in range(1, bits, 2)]

    def summed_over_sections(value):
        parts = [value]
        for steps in rounds:
            value = parts[0]
            for part in parts[1:]:
                value = value + part
            parts = [value] + [sent_to(value, lambda s, m, k=k: (s ^ k, m)) for k in steps]
        return parts

    first = packed_from_hbm(block, thin, packed)
    lower_sent, first = lax.optimization_barrier((lower, first))
    packed_down = sent_to(first, lambda s, m: (s + 1, m) if parity(s + 1, m) else None)

    def needs_lower(s, m):
        return m == home(s) or (s + 2 < sections and m == home(s + 2))

    lower_down = sent_to(lower_sent, lambda s, m: (s + 1, m) if s >= 1 and needs_lower(s + 1, m) else None)
    lower_up = sent_to(lower_sent, lambda s, m: (s - 1, m) if s >= 1 and m == home(s - 1) else None)
    up = call(
        first_own_kernel,
        [packed],
        [stacked, stacked, square, square, thin_shape],
        (first, lower),
        6 * product,
        hbm=1,
    )
    up = sent_to(up, lambda s, m: (s - 1, m) if parity(s - 1, m) else None)
    other = sent_to(local, lambda s, m: (s, m ^ 1))
    through, full = call(
        first_receive_kernel, [square, stacked], [stacked, square, square], (packed_down, lower), 6 * long, hbm=1
    )
    sent, block, thin = call(fold_kernel, [packed, square, thin_shape], [], (first, full, up), 0)

    packed_down = sent_to(sent, lambda s, m: (s + 2, m) if m == home(s + 2) else None)
    up, done = call(
        bracket_kernel, [packed, (8, TILE)], [stacked, stacked], (block, thin, through), 6 * product
    )
    early = sent_to(up, lambda s, m: (s - 2, m) if m == home(s - 2) and m != home(s) else None)
    up_late = up
    lower_down, other = lax.optimization_barrier((lower_down, other))
    lower = call(lower_kernel, [square], [], (through, lower_down, done), product)
    lower_down = sent_to(lower, lambda s, m: (s + 2, m) if s >= 2 and m == home(s + 2) else None)
    up_late, _ = lax.optimization_barrier((up_late, lower))
    late = sent_to(up_late, lambda s, m: (s - 2, m) if m == home(s - 2) and m == home(s) else None)
    packed_down, lower_up = lax.optimization_barrier((packed_down, lower_up))
    through, full = call(receive_kernel, [square, stacked], [stacked, square], (packed_down, lower), 6 * product)
    has_before = lambda: lax.axis_index("sec") >= 4
    if sections == 8:
        block_kept, thin_kept, inverse = call(
            functools.partial(fold_kept_kernel, has_before),
            [square, thin_shape, square],
            [stacked, stacked, square],
            (early, lower_up, block, thin, full),
            2 * long,
        )
        sent, block, thin = call(
            functools.partial(fold_sent_kernel, lambda: lax.axis_index("sec") < 4),
            [packed, square, thin_shape],
            [stacked, stacked, square, packed],
            (thin_kept, early, late, lower_up, block, thin, full),
            3 * long,
        )
    else:
        sent, block, thin = call(
            fold_above_kernel,
            [packed, square, thin_shape],
            [stacked, stacked, square, packed],
            (early, late, lower_up, block, thin, full),
            2 * long,
        )
        inverse = call(functools.partial(whole_inverse_kernel, has_before), [square], [], (block,), 4 * long)
        block_kept, thin_kept = block, thin

    sent, lower_down = lax.optimization_barrier((sent, lower_down))
    packed_down = sent_to(sent, lambda s, m: (s + 4, home(s + 4)) if m == home(s) else None)
    lower, up = call(
        functools.partial(last_lower_kernel, has_before), [square, packed], [stacked, stacked], (through, lower_down, inverse, thin_kept), 3 * product
    )
    up = sent_to(up, lambda s, m: (s - 4, home(s - 4)) if m == home(s) else None)
    block, thin = call(
        functools.partial(last_receive_kernel, has_before),
        [square, thin_shape],
        [stacked, square],
        (packed_down, lower, block_kept, thin_kept, block, thin),
        6 * product,
    )
    solved = call(solve_kernel, [thin_shape], [square, thin_shape], (block, thin, up), product)

    parts = [
        sent_to(solved, lambda s, m, k=k: (s, (m + k) % groups) if m == home(s) else None)
        for k in range(1, groups)
    ]
    whole, payload = call(
        functools.partial(modal_kernel, home),
        [thin_shape, (columns + 2 * sections, 2 * modes.shape[2])],
        [],
        (solved, *parts, local, other),
        product // 32,
    )
    parts = summed_over_sections(payload)
    keep, give = call(
        functools.partial(back_kernel_of, len(parts)),
        [(columns, width)] * 2,
        [thin_shape],
        (*parts, local, other),
        product // 32,
    )
    summed = keep + sent_to(give, lambda s, m: (s, m ^ 2))
    own_columns = lax.dynamic_slice_in_dim(whole, lax.axis_index("mode") * width, width, 1)
    return (own_columns[None], (own_columns - summed)[None])


def solution(mesh):
    in_specs = (
        P("sec", None, None),
        P("sec", None, None),
        P("sec", None, None),
        P("sec", None, "mode"),
        P("sec"),
        P("sec"),
        P("sec", "mode"),
    )
    out_specs = (P("sec", None, "mode"), P("sec", None, "mode"))
    return jax.shard_map(
        per_device, mesh=mesh, in_specs=in_specs, out_specs=out_specs, check_vma=False
    )
```

```python
import functools

import jax
import jax.numpy as jnp
from jax import lax
from jax.experimental import pallas as pl
from jax.experimental.pallas import tpu as pltpu
from jax.sharding import PartitionSpec as P

LEVELS = 3
BUCKET = 64
RATES = (0.2, 0.5, 1.0, 2.0)
AXES = ("sec", "mode")
TILE = 128
f32, bf16 = jnp.float32, jnp.bfloat16


def split(value):
    high = value.astype(bf16)
    return high, (value - high.astype(f32)).astype(bf16)


def dot(left, right):
    return jnp.dot(left, right, preferred_element_type=f32)


def dot_t(left, right):
    return lax.dot_general(left, right, (((1,), (1,)), ((), ())), preferred_element_type=f32)


def times(left, right, product=dot):
    return product(left[0], right[0]) + product(left[0], right[1]) + product(left[1], right[0])


def upper(size):
    count = size // TILE
    return [(a, b) for a in range(count) for b in range(a, count)]


def band(index):
    return slice(TILE * index, TILE * index + TILE)


def unpack(packed, block, thin):
    size = block.shape[0]
    cells = upper(size)
    for index, (a, b) in enumerate(cells):
        cell = packed[band(index), :]
        block[band(a), band(b)] = cell
        if a != b:
            block[band(b), band(a)] = cell.T
    rows = thin.shape[0]
    for c in range(size // TILE):
        start = TILE * len(cells) + rows * c
        thin[:, band(c)] = packed[start : start + rows, :]


def pack(packed, block, thin):
    size = block.shape[1]
    cells = upper(size)
    for index, (a, b) in enumerate(cells):
        packed[band(index), :] = block[band(a), band(b)]
    rows = thin.shape[0]
    for c in range(size // TILE):
        start = TILE * len(cells) + rows * c
        packed[start : start + rows, :] = thin[:, band(c)]


def scaled(block):
    size = block.shape[0]
    eye = lax.broadcasted_iota(jnp.int32, (size, size), 0) == lax.broadcasted_iota(
        jnp.int32, (size, size), 1
    )
    only = jnp.where(eye, block, 0.0)
    down = jnp.sum(only, axis=1, keepdims=True)
    along = jnp.sum(only, axis=0, keepdims=True)
    down = jnp.where(down == 0.0, 0.0, 1.0 / down)
    along = jnp.where(along == 0.0, 0.0, 1.0 / along)
    unit = jnp.where(eye, 1.0, 0.0)
    return unit, down, along, unit - down * block


def inverse_of(block):
    unit, down, along, first = scaled(block)
    one = split(first)
    second = times(one, one)
    two = split(second)
    third = dot(one[0], two[0])
    fourth = dot(two[0], two[0]).astype(bf16)
    series = unit + first + second + third
    series = series + dot(series.astype(bf16), fourth)
    return series * along


def schur(rows_and_thin, inverse, right, product):
    through = times(split(rows_and_thin), split(inverse))
    return through, times(split(through), split(right), product)


def pack_kernel(block, thin, packed, sems):
    size = block.shape[0]
    cells = upper(size)
    rows = thin.shape[0]
    pairs = [
        (block.at[band(a), band(b)], packed.at[band(index), :]) for index, (a, b) in enumerate(cells)
    ]
    for c in range(size // TILE):
        start = TILE * len(cells) + rows * c
        pairs.append((thin.at[:, band(c)], packed.at[start : start + rows, :]))
    copies = [pltpu.make_async_copy(src, dst, sems.at[k]) for k, (src, dst) in enumerate(pairs)]
    for copy in copies:
        copy.start()
    for copy in copies:
        copy.wait()


def folded(packed, block, thin, *others):
    size = block.shape[0]
    cells = upper(size)
    for index, (a, b) in enumerate(cells):
        value = block[band(a), band(b)]
        for other in others:
            same = other.shape == packed.shape
            value = value - (other[band(index), :] if same else other[band(a), band(b)])
        packed[band(index), :] = value
    rows = thin.shape[0]
    for c in range(size // TILE):
        start = TILE * len(cells) + rows * c
        value = thin[:, band(c)]
        for other in others:
            same = other.shape == packed.shape
            value = value - (other[start : start + rows, :] if same else other[size:, band(c)])
        packed[start : start + rows, :] = value


def first_own_kernel(both, lower_hbm, packed, stack, out, lower, whole, thin, sem):
    copy = pltpu.make_async_copy(lower_hbm, lower, sem)
    copy.start()
    unpack(both, whole, thin)
    own_kernel(whole, thin, lower, packed, stack, out, copy)


def own_kernel(block, thin, lower, packed, stack, out, copy=None):
    size = block.shape[0]
    inverse = inverse_of(block[...])
    if copy is not None:
        copy.wait()
    stack[0:size, :] = lower[...].T
    stack[size:, :] = thin[...]
    _, out[...] = schur(stack[...], inverse, lower[...], dot)
    pack(packed, out, out.at[size:, :])


def bracket_kernel(block, thin, lower, packed, done, stack, out):
    own_kernel(block, thin, lower, packed, stack, out)
    done[...] = jnp.zeros_like(done)


def first_receive_kernel(packed, lower_hbm, through, full, stack, whole, lower, sem):
    copy = pltpu.make_async_copy(lower_hbm, lower, sem)
    copy.start()
    receive_kernel(packed, lower, through, full, stack, whole, copy)


def receive_kernel(packed, lower, through, full, stack, whole, copy=None):
    size = lower.shape[0]
    unpack(packed, whole, stack.at[size:, :])
    inverse = inverse_of(whole[...])
    if copy is not None:
        copy.wait()
    stack[0:size, :] = lower[...]
    half, full[...] = schur(stack[...], inverse, lower[...], dot_t)
    through[...] = half[0:size, :]


def fold_kernel(both, full, above, packed, block_out, thin_out):
    unpack(both, block_out, thin_out)
    folded(packed, block_out, thin_out, full, above)
    unpack(packed, block_out, thin_out)


def part_above(packed_above, passed, stack, out, whole):
    size = passed.shape[0]
    unpack(packed_above, whole, stack.at[size:, :])
    right = split(passed[...])
    stack[0:size, :] = times(split(passed[...].T), split(whole[...]))
    stack[size:, :] = -stack[size:, :]
    out[...] = times(split(stack[...]), right)


def fold_above_kernel(early, late, passed, block, thin, full, packed, block_out, thin_out, stack, out, whole, both):
    both[...] = early[...] + late[...]
    part_above(both, passed, stack, out, whole)
    folded(packed, block, thin, full, out)
    unpack(packed, block_out, thin_out)


def fold_sent_kernel(needed, after, early, late, passed, block, thin, full, packed, block_out, thin_out, *scratch):
    @pl.when(needed())
    def _():
        fold_above_kernel(early, late, passed, block, thin, full, packed, block_out, thin_out, *scratch)


def fold_kept_kernel(needed, early, passed, block, thin, full, block_out, thin_out, inverse, stack, out, whole):
    size = block.shape[0]

    @pl.when(needed())
    def _():
        part_above(early, passed, stack, out, whole)
        value = block[...] - full[0:size, :] - out[0:size, :]
        block_out[...] = value
        thin_out[...] = thin[...] - full[size:, :] - out[size:, :]
        inverse[...] = inverse_of(value)


def whole_inverse_kernel(needed, block, inverse):
    @pl.when(needed())
    def _():
        inverse[...] = inverse_of(block[...])


def lower_kernel(through, passed, after, lower):
    lower[...] = -times(split(through[...]), split(passed[...]))


def last_lower_kernel(needed, through, passed, inverse, thin, lower, packed, stack, out):
    size = inverse.shape[0]

    @pl.when(needed())
    def _():
        value = -times(split(through[...]), split(passed[...]))
        lower[...] = value
        stack[0:size, :] = value.T
        stack[size:, :] = thin[...]
        _, out[...] = schur(stack[...], inverse[...], value, dot)
        pack(packed, out, out.at[size:, :])


def last_receive_kernel(needed, packed, lower, block, thin, block_else, thin_else, block_out, thin_out, stack, whole):
    size = block.shape[0]

    @pl.when(needed())
    def _():
        unpack(packed, whole, stack.at[size:, :])
        inverse = inverse_of(whole[...])
        stack[0:size, :] = lower[...]
        _, full = schur(stack[...], inverse, lower[...], dot_t)
        block_out[...] = block[...] - full[0:size, :]
        thin_out[...] = thin[...] - full[size:, :]

    @pl.when(jnp.logical_not(needed()))
    def _():
        block_out[...] = block_else[...]
        thin_out[...] = thin_else[...]


def solve_kernel(block, thin, above, solution, whole, own):
    unpack(above, whole, own)
    value = block[...] - whole[...]
    unit, _, along, _ = scaled(value)
    high, low = split(unit - value * along)
    rows = thin.shape[0]
    now = (thin[...] - own[...]) * along
    for power in (1, 2, 4):
        moved = now
        for _ in range(power):
            top, rest = split(moved)
            both = dot(jnp.concatenate([top, rest], axis=0), high)
            moved = both[0:rows, :] + both[rows:, :] + dot(top, low)
        now = now + moved
    solution[...] = now


def shares_kernel(regime, joints, participation, modes, out):
    depth = modes.shape[0]
    sections, count = out.shape[0] - depth, joints.shape[1]
    out[0:depth, :] = modes[...].astype(f32)
    bucket = lax.broadcasted_iota(jnp.int32, (1, count), 1) // BUCKET
    rate = jnp.zeros((1, count), f32)
    for b in range(count // BUCKET):
        value = jnp.float32(0.0)
        for index, known in enumerate(RATES):
            value = jnp.where(regime[b] == index, jnp.float32(known), value)
        rate = jnp.where(bucket == b, value, rate)
    section = lax.broadcasted_iota(jnp.int32, (sections, count), 0)
    weights = jnp.where(section == joints[...], rate, 0.0)
    squares = participation[...].astype(f32)
    out[depth:, :] = times(split(weights), split(squares * squares))


def modal_kernel(home, a, b, c, d, local, other, whole, payload):
    position, plane = lax.axis_index("sec"), lax.axis_index("mode")
    own = jnp.where(home(position) == plane, a[...], 0.0)
    value = own + b[...] + c[...] + d[...]
    whole[...] = value
    amplitude = jnp.sqrt(jnp.sum(value * value, keepdims=True) / value.size + 1e-06)
    (rows, depth), width = value.shape, local.shape[1]
    sections = local.shape[0] - depth
    rounded = value.astype(bf16)
    for k, source in enumerate((local, other)):
        columns = slice(width * k, width * k + width)
        payload[0:rows, columns] = dot(rounded, source[0:depth, :].astype(bf16))
        payload[rows : rows + sections, columns] = source[depth:, :]
    mine = lax.broadcasted_iota(jnp.int32, (sections, 2 * width), 0) == position
    payload[rows + sections :, :] = jnp.where(mine, amplitude / (1.0 + amplitude), 0.0)


def back_kernel_of(count, *refs):
    plane = lax.axis_index("mode")
    parts, (local, other), (keep, give), scratch = refs[:count], refs[count : count + 2], refs[count + 2 : -1], refs[-1]
    total = parts[0][...]
    for part in parts[1:]:
        total = total + part[...]
    rows, depth = scratch.shape
    sections = (total.shape[0] - rows) // 2
    products = total[rows : rows + sections, :] * total[rows + sections :, :]
    damping = jnp.sum(products, axis=0, keepdims=True)
    removed = (total[0:rows, :] * (damping / (1.0 + damping))).astype(bf16)
    half = local.shape[1]
    scratch[...] = dot_t(removed[:, 0:half], local[0:depth, :].astype(bf16)) + dot_t(
        removed[:, half:], other[0:depth, :].astype(bf16)
    )
    width = keep.shape[1]
    for out, owner in ((keep, plane), (give, plane ^ 2)):
        out[...] = scratch[:, pl.ds(pl.multiple_of(owner * width, width), width)]


def packed_from_hbm(block, thin, packed):
    cells = len(upper(block.shape[0])) + block.shape[0] // TILE
    return pl.pallas_call(
        pack_kernel,
        out_shape=pltpu.VMEM(packed, f32),
        in_specs=[pl.BlockSpec(memory_space=pl.ANY)] * 2,
        out_specs=pl.BlockSpec(memory_space=pltpu.VMEM),
        scratch_shapes=[pltpu.SemaphoreType.DMA((cells,))],
    )(block, thin)


def call(kernel, outs, scratch, args, flops, smem=0, hbm=0):
    vmem, scalar = pl.BlockSpec(memory_space=pltpu.VMEM), pl.BlockSpec(memory_space=pltpu.SMEM)
    moved = sum(a.size * a.dtype.itemsize for a in args) + sum(4 * o[0] * o[1] for o in outs)
    single = len(outs) == 1
    shapes = [jax.ShapeDtypeStruct(o, f32) for o in outs]
    return pl.pallas_call(
        kernel,
        out_shape=shapes[0] if single else tuple(shapes),
        in_specs=[scalar] * smem
        + [vmem] * (len(args) - smem - hbm)
        + [pl.BlockSpec(memory_space=pl.ANY)] * hbm,
        out_specs=vmem if single else tuple([vmem] * len(outs)),
        scratch_shapes=[pltpu.VMEM(s, f32) for s in scratch] + [pltpu.SemaphoreType.DMA] * hbm,
        compiler_params=pltpu.CompilerParams(vmem_limit_bytes=14 << 20),
        cost_estimate=pl.CostEstimate(flops=int(flops), transcendentals=0, bytes_accessed=moved),
    )(*args)


def per_device(coupling, stiffness, loads, modes, joint_section, regime, participation):
    sections, groups = lax.axis_size("sec"), lax.axis_size("mode")
    assert groups == 4 and LEVELS == 3
    size, columns = stiffness.shape[1], loads.shape[1]
    width = size // groups
    cells = len(upper(size))
    packed = (TILE * cells + columns * (size // TILE), TILE)
    square, stacked, thin_shape = (size, size), (size + columns, size), (columns, size)
    product = 0.1 * 6 * size**3
    long = 1.0 * 6 * size**3

    def sent_to(value, where):
        pairs = []
        for s in range(sections):
            for m in range(groups):
                to = where(s, m)
                if to is not None and 0 <= to[0] < sections:
                    pairs.append((s * groups + m, to[0] * groups + to[1]))
        return lax.ppermute(value, AXES, pairs)

    def home(s):
        return 2 * (s % 2) + (s // 2 + s // 4) % 2

    def parity(s, m):
        return m // 2 == s % 2

    block, thin, lower = stiffness[0], loads[0], coupling[0]

    local = call(
        shares_kernel,
        [(size + sections, participation.shape[1])],
        [],
        (regime, joint_section[None, :], participation, modes[0]),
        product // 32,
        smem=1,
    )
    bits = sections.bit_length() - 1
    rounds = [[1]] + [[1 << b, 2 << b, 3 << b] if b + 1 < bits else [1 << b] for b in range(1, bits, 2)]

    def summed_over_sections(value):
        parts = [value]
        for steps in rounds:
            value = parts[0]
            for part in parts[1:]:
                value = value + part
            parts = [value] + [sent_to(value, lambda s, m, k=k: (s ^ k, m)) for k in steps]
        return parts

    first = packed_from_hbm(block, thin, packed)
    lower_sent, first = lax.optimization_barrier((lower, first))
    packed_down = sent_to(first, lambda s, m: (s + 1, m) if parity(s + 1, m) else None)

    def needs_lower(s, m):
        return m == home(s) or (s + 2 < sections and m == home(s + 2))

    lower_down = sent_to(lower_sent, lambda s, m: (s + 1, m) if s >= 1 and needs_lower(s + 1, m) else None)
    lower_up = sent_to(lower_sent, lambda s, m: (s - 1, m) if s >= 1 and m == home(s - 1) else None)
    up = call(
        first_own_kernel,
        [packed],
        [stacked, stacked, square, square, thin_shape],
        (first, lower),
        6 * product,
        hbm=1,
    )
    up = sent_to(up, lambda s, m: (s - 1, m) if parity(s - 1, m) else None)
    other = sent_to(local, lambda s, m: (s, m ^ 1))
    through, full = call(
        first_receive_kernel, [square, stacked], [stacked, square, square], (packed_down, lower), 6 * long, hbm=1
    )
    sent, block, thin = call(fold_kernel, [packed, square, thin_shape], [], (first, full, up), 0)

    packed_down = sent_to(sent, lambda s, m: (s + 2, m) if m == home(s + 2) else None)
    up, done = call(
        bracket_kernel, [packed, (8, TILE)], [stacked, stacked], (block, thin, through), 6 * product
    )
    early = sent_to(up, lambda s, m: (s - 2, m) if m == home(s - 2) and m != home(s) else None)
    up_late = up
    lower_down, other = lax.optimization_barrier((lower_down, other))
    lower = call(lower_kernel, [square], [], (through, lower_down, done), product)
    lower_down = sent_to(lower, lambda s, m: (s + 2, m) if s >= 2 and m == home(s + 2) else None)
    up_late, _ = lax.optimization_barrier((up_late, lower))
    late = sent_to(up_late, lambda s, m: (s - 2, m) if m == home(s - 2) and m == home(s) else None)
    packed_down, lower_up = lax.optimization_barrier((packed_down, lower_up))
    through, full = call(receive_kernel, [square, stacked], [stacked, square], (packed_down, lower), 6 * product)
    has_before = lambda: lax.axis_index("sec") >= 4
    if sections == 8:
        block_kept, thin_kept, inverse = call(
            functools.partial(fold_kept_kernel, has_before),
            [square, thin_shape, square],
            [stacked, stacked, square],
            (early, lower_up, block, thin, full),
            2 * long,
        )
        sent, block, thin = call(
            functools.partial(fold_sent_kernel, lambda: lax.axis_index("sec") < 4),
            [packed, square, thin_shape],
            [stacked, stacked, square, packed],
            (thin_kept, early, late, lower_up, block, thin, full),
            3 * long,
        )
    else:
        sent, block, thin = call(
            fold_above_kernel,
            [packed, square, thin_shape],
            [stacked, stacked, square, packed],
            (early, late, lower_up, block, thin, full),
            2 * long,
        )
        inverse = call(functools.partial(whole_inverse_kernel, has_before), [square], [], (block,), 4 * long)
        block_kept, thin_kept = block, thin

    sent, lower_down = lax.optimization_barrier((sent, lower_down))
    packed_down = sent_to(sent, lambda s, m: (s + 4, home(s + 4)) if m == home(s) else None)
    lower, up = call(
        functools.partial(last_lower_kernel, has_before), [square, packed], [stacked, stacked], (through, lower_down, inverse, thin_kept), 3 * product
    )
    up = sent_to(up, lambda s, m: (s - 4, home(s - 4)) if m == home(s) else None)
    block, thin = call(
        functools.partial(last_receive_kernel, has_before),
        [square, thin_shape],
        [stacked, square],
        (packed_down, lower, block_kept, thin_kept, block, thin),
        6 * product,
    )
    solved = call(solve_kernel, [thin_shape], [square, thin_shape], (block, thin, up), product)

    parts = [
        sent_to(solved, lambda s, m, k=k: (s, (m + k) % groups) if m == home(s) else None)
        for k in (3, 2, 1)
    ]
    whole, payload = call(
        functools.partial(modal_kernel, home),
        [thin_shape, (columns + 2 * sections, 2 * modes.shape[2])],
        [],
        (solved, *parts, local, other),
        product // 32,
    )
    parts = summed_over_sections(payload)
    keep, give = call(
        functools.partial(back_kernel_of, len(parts)),
        [(columns, width)] * 2,
        [thin_shape],
        (*parts, local, other),
        product // 32,
    )
    summed = keep + sent_to(give, lambda s, m: (s, m ^ 2))
    own_columns = lax.dynamic_slice_in_dim(whole, lax.axis_index("mode") * width, width, 1)
    return (own_columns[None], (own_columns - summed)[None])


def solution(mesh):
    in_specs = (
        P("sec", None, None),
        P("sec", None, None),
        P("sec", None, None),
        P("sec", None, "mode"),
        P("sec"),
        P("sec"),
        P("sec", "mode"),
    )
    out_specs = (P("sec", None, "mode"), P("sec", None, "mode"))
    return jax.shard_map(
        per_device, mesh=mesh, in_specs=in_specs, out_specs=out_specs, check_vma=False
    )
```
